256 devices in a mesh: prow: 8 (over z_hi, y), pcol: 32 (over x, z_lo, core).
Axes of the slice: x: 4, y: 4, z: 8 (z_hi: 2, z_lo: 4; z = z_hi * 4 + z_lo), core: 2. Of those that a mesh axis runs over, the one named last changes fastest.
Arguments:
- inverse_blocks: float32 [12288, 12288], P('pcol', 'prow')
- panel_first: float32 [12288, 384], P('prow'), may hold values from -0.0546875 to 0.0546875
- panel_second: float32 [12288, 384], P('pcol'), may hold values from -0.0546875 to 0.0546875
- panel_link: float32 [384, 384], replicated, may hold values from -0.3125 to 0.3125
- diag_inverse: float32 [384, 384], replicated
- ancestors: int32 [2, 32], replicated, may hold values from 0 to 1, as said below
Outputs:
- column_first: float32 [12288, 384], P('pcol')
- diag_first: float32 [384, 384], replicated
- column_second: float32 [12288, 384], P(('prow', 'pcol'))
- corner: float32 [384, 384], replicated
The draws below stay inside these ranges and needn't reach their ends.
Inputs may be any that keep to these rules, and one draw needn't show every extreme that they name: `ancestors`: every block marked in row 1 is also marked in row 0; `inverse_blocks` is symmetric (equal to its transpose).
All inputs are finite; a program needn't handle non-finite values.
Results may differ from the reference program's by a relative error of at most 0.0001.
Values sent between devices are 32-bit elements; how exact they have to be, the bound alone decides.
A program may use at most 64 MiB of HBM per device.

```python
import jax
import jax.numpy as jnp
from jax import lax

B = 384
NB = 32
N = 12288


def draw_inverse_blocks(key, part):
    base = jax.random.normal(jax.random.fold_in(key, 11), (N, N), jnp.float32)
    sym = (base + base.T) * 0.7071
    return sym


def draw_diag_inverse(key, part):
    base = jax.random.normal(jax.random.fold_in(key, 21), (B, B), jnp.float32)
    return jnp.eye(B, dtype=jnp.float32) + (base + base.T) * (0.5 / B ** 0.5)


def draw_ancestors(key, part):
    first = (jax.random.randint(jax.random.fold_in(key, 31), (NB,), 0, 5) < 3).astype(jnp.int32)
    keep = (jax.random.randint(jax.random.fold_in(key, 32), (NB,), 0, 5) < 3).astype(jnp.int32)
    position = jnp.arange(NB)
    forced = ((position == 0) | (position == NB // 2)).astype(jnp.int32)
    first = jnp.maximum(first, forced)
    keep = jnp.maximum(keep, forced)
    return jnp.stack([first, first * keep])


def levels(key, dims, pieces, low, top_value):
    def one(axis_at, blocks):
        draws = jax.random.uniform(jax.random.fold_in(jax.random.fold_in(key, 6), axis_at), (blocks,), jnp.float32, low / len(pieces), top_value / len(pieces))
        return jnp.repeat(jnp.exp(draws), dims[axis_at] // blocks).reshape((-1,) + (1,) * (len(dims) - axis_at - 1))

    factor_of = one(*pieces[0])
    for cut in pieces[1:]:
        factor_of = factor_of * one(*cut)
    return factor_of


def centred(stream_key, extent, deviation, limit, pieces=(), kind=jnp.bfloat16):
    result = jax.random.normal(stream_key, extent, jnp.float32) * deviation
    if len(pieces) > 0:
        result = levels(stream_key, extent, pieces, -0.22, 0.18) * result
    return jnp.clip(result, min=-limit, max=limit).astype(kind)


def setup_inputs(seed: int = 0) -> dict:
    streams_of = jax.random.split(jax.random.key(seed), 7)
    return {
        "inverse_blocks": draw_inverse_blocks(jax.random.fold_in(streams_of[6], 71), 0),
        "panel_first": centred(streams_of[1], (N, B), N ** -0.5, 0.0546875, ((0, 8),), jnp.float32),
        "panel_second": centred(streams_of[2], (N, B), N ** -0.5, 0.0546875, ((0, 32),), jnp.float32),
        "panel_link": centred(streams_of[3], (B, B), B ** -0.5, 0.3125, (), jnp.float32),
        "diag_inverse": draw_diag_inverse(jax.random.fold_in(streams_of[6], 71), 0),
        "ancestors": draw_ancestors(jax.random.fold_in(streams_of[6], 71), 0),
    }


def product(left, right):
    return jnp.dot(left, right, precision=lax.Precision.HIGHEST, preferred_element_type=jnp.float32)


def reference(inverse_blocks, panel_first, panel_second, panel_link, diag_inverse, ancestors):
    marks = ancestors.astype(jnp.float32)
    first = jnp.repeat(marks[0], B)[:, None]
    second = jnp.repeat(marks[1], B)[:, None]
    column_first = -first * product(inverse_blocks, first * panel_first)
    diag_first = diag_inverse - product((first * panel_first).T, column_first)
    column_second = -second * (product(inverse_blocks, second * panel_second) + product(column_first, panel_link))
    corner = -(product((second * column_first).T, panel_second) + product(diag_first, panel_link))
    return column_first, diag_first, column_second, corner
```

```python
import functools

import jax
import jax.numpy as jnp
from jax import lax
from jax.experimental import pallas as pl
from jax.experimental.pallas import tpu as pltpu
from jax.sharding import PartitionSpec as P

MESH = pl.DeviceIdType.MESH
F32 = jnp.float32
BF16 = jnp.bfloat16
B = 384
CH = 3
W = 128
H = 48
S = 16
ROWS = (((0,), (0,)), ((), ()))
PLAIN = (((1,), (0,)), ((), ()))


def split(value):
    high = value.astype(BF16)
    low = (value - high.astype(F32)).astype(BF16)
    return high, low


def mul(left, right, dims=PLAIN):
    return lax.dot_general(left, right, dims, preferred_element_type=F32)


def product(left, right, dims=PLAIN):
    left_high, left_low = left
    right_high, right_low = right
    return mul(left_high, right_high, dims) + (mul(left_high, right_low, dims) + mul(left_low, right_high, dims))


class Copies:
    def __init__(self, send_sems, recv_sems):
        self.send_sems, self.recv_sems = send_sems, recv_sems
        self.sends, self.recvs, self.sent = {}, {}, []

    def slot(self, table, key):
        if key not in table:
            table[key] = len(table)
        return table[key]

    def make(self, key, src, dst, device, send_key=None):
        send = self.slot(self.sends, key if send_key is None else send_key)
        recv = self.slot(self.recvs, key)
        return pltpu.make_async_remote_copy(
            src_ref=src,
            dst_ref=dst,
            send_sem=self.send_sems.at[send],
            recv_sem=self.recv_sems.at[recv],
            device_id=device,
            device_id_type=MESH,
        )

    def send(self, key, src, dst, device):
        copy = self.make(key, src, dst, device)
        copy.start()
        self.sent.append(copy)

    def wait(self, key, dst, device):
        self.make(key, dst, dst, device).wait_recv()

    def finish(self):
        for copy in self.sent:
            copy.wait_send()


class Ring:
    def __init__(self, copies, name, pos, plus, minus, get):
        self.copies, self.name, self.pos, self.plus, self.minus, self.get = copies, name, pos, plus, minus, get

    def at(self, offset, half):
        return self.get(lax.rem(self.pos + offset, 4), half)


class Scatter(Ring):
    def __init__(self, copies, name, pos, plus, minus, get, relay, direct, final):
        super().__init__(copies, name, pos, plus, minus, get)
        self.relayed, self.direct, self.final = relay, direct, final

    def start_far(self):
        self.copies.send((self.name, 0), self.at(2, 0), self.relayed(0), self.plus)
        self.copies.send((self.name, 1), self.at(2, 1), self.relayed(1), self.minus)

    def start_plus(self):
        self.copies.send((self.name, 2), self.at(1, 1), self.direct(0), self.plus)

    def start_minus(self):
        self.copies.send((self.name, 3), self.at(3, 0), self.direct(1), self.minus)

    def relay(self):
        self.copies.wait((self.name, 0), self.relayed(0), self.minus)
        mine = self.at(1, 0)
        mine[...] = mine[...] + self.relayed(0)[...]
        self.copies.send((self.name, 4), mine, self.final(0), self.plus)
        self.copies.wait((self.name, 1), self.relayed(1), self.plus)
        mine = self.at(3, 1)
        mine[...] = mine[...] + self.relayed(1)[...]
        self.copies.send((self.name, 5), mine, self.final(1), self.minus)

    def finish(self):
        self.copies.wait((self.name, 2), self.direct(0), self.minus)
        self.copies.wait((self.name, 3), self.direct(1), self.plus)
        self.copies.wait((self.name, 4), self.final(0), self.minus)
        self.copies.wait((self.name, 5), self.final(1), self.plus)
        first = self.at(0, 0)[...] + (self.direct(1)[...] + self.final(0)[...])
        second = self.at(0, 1)[...] + (self.direct(0)[...] + self.final(1)[...])
        return first, second


class Gather(Ring):
    def start(self):
        for number, half, device in ((0, 0, self.plus), (1, 1, self.minus), (2, 1, self.plus), (3, 0, self.minus)):
            self.copies.send((self.name, number), self.at(0, half), self.at(0, half), device)

    def relay(self):
        self.copies.wait((self.name, 0), self.at(3, 0), self.minus)
        self.copies.send((self.name, 4), self.at(3, 0), self.at(3, 0), self.plus)
        self.copies.wait((self.name, 1), self.at(1, 1), self.plus)
        self.copies.send((self.name, 5), self.at(1, 1), self.at(1, 1), self.minus)

    def near(self):
        self.copies.wait((self.name, 2), self.at(3, 1), self.minus)
        self.copies.wait((self.name, 3), self.at(1, 0), self.plus)

    def far(self):
        self.copies.wait((self.name, 4), self.at(2, 0), self.minus)
        self.copies.wait((self.name, 5), self.at(2, 1), self.plus)


def kernel(
    marks, inv, pan1, pan2, link, diag, column_first, diag_first, column_second, corner,
    inv_high, inv_low, pan1_cat, pan2_cat, link_high, link_low, base,
    part, part_relay, part_direct, part_final, quarter, quarter_in, column,
    wide, wide_in, wide_relay, wide_direct, wide_final, mine, mine_in, link_rows,
    turned, turned_in, cross, pair, pair_in, slices, slices_in, depth, grid,
    send_sems, recv_sems,
):
    row, col = lax.axis_index("prow"), lax.axis_index("pcol")
    y, zh = lax.rem(row, 4), lax.div(row, 4)
    x, zl, core = lax.div(col, 8), lax.rem(lax.div(col, 2), 4), lax.rem(col, 2)
    z = zh * 4 + zl

    def device(y=y, zh=zh, x=x, zl=zl, core=core):
        return (zh * 4 + y, (x * 4 + zl) * 2 + core)

    def turn(value, step, size=4):
        return lax.rem(value + step, size)

    def along_z(step):
        there = turn(z, step, 8)
        return device(zh=lax.div(there, 4), zl=lax.rem(there, 4))

    y_plus, y_minus = device(y=turn(y, 1)), device(y=turn(y, 3))
    x_plus, x_minus, x_far = device(x=turn(x, 1)), device(x=turn(x, 3)), device(x=turn(x, 2))
    partner = device(core=1 - core)
    owner_row = lax.div(col, 4)
    is_owner = row == owner_row

    gives = zh == lax.div(col, 16)

    def taker(half):
        return (owner_row, lax.rem(col, 4) * 8 + y * 2 + half)

    def is_self(half):
        there = taker(half)
        return jnp.logical_and(there[0] == row, there[1] == col)

    giver = (zh * 4 + lax.div(lax.rem(col, 8), 2), row * 4 + lax.div(col, 8))
    from_self = jnp.logical_and(giver[0] == row, giver[1] == col)

    barrier = pltpu.get_barrier_semaphore()

    def greet(there):
        pl.semaphore_signal(barrier, inc=1, device_id=there, device_id_type=MESH)

    for there in (y_plus, y_minus, x_plus, x_minus, x_far, partner):
        greet(there)
    for step in range(1, 8):
        greet(along_z(step))

    @pl.when(jnp.logical_not(from_self))
    def _():
        greet(giver)

    @pl.when(jnp.logical_not(is_owner))
    def _():
        greet((owner_row, col))

    copies = Copies(send_sems, recv_sems)

    first_own = marks[0, col].astype(F32)
    second_own = marks[1, col].astype(F32)
    for block in range(4):
        at = pl.ds(block * B, B)
        scaled = pan1[at, :] * marks[0, row * 4 + block].astype(F32)
        high, low = split(scaled)
        for chunk in range(CH):
            lanes = slice(chunk * W, (chunk + 1) * W)
            pan1_cat[chunk, at, 0:W] = high[:, lanes]
            pan1_cat[chunk, at, W : 2 * W] = low[:, lanes]
        inv_high[:, at], inv_low[:, at] = split(inv[:, at])

    ring = []
    for chunk in range(CH):
        ring.append(
            Scatter(
                copies, ("part", chunk), y, y_plus, y_minus,
                lambda q, h, chunk=chunk: part.at[chunk, q, h],
                lambda h, chunk=chunk: part_relay.at[chunk, h],
                lambda h, chunk=chunk: part_direct.at[chunk, h],
                lambda h, chunk=chunk: part_final.at[chunk, h],
            )
        )

    def partial_product(chunk):
        both = mul(inv_high[...], pan1_cat[chunk])
        rest = mul(inv_low[...], pan1_cat[chunk, :, 0:W])
        total = (both[:, 0:W] + (both[:, W : 2 * W] + rest)) * (-first_own)
        part[chunk] = total.reshape(4, 2, H, W)

    def start_ring(chunk):
        ring[chunk].start_far()
        ring[chunk].start_plus()
        ring[chunk].start_minus()

    partial_product(0)
    waits = 13 + jnp.where(is_owner, 7, 0)
    for half in range(2):
        waits = waits + jnp.where(jnp.logical_and(gives, jnp.logical_not(is_self(half))), 1, 0)
    pl.semaphore_wait(barrier, waits)
    start_ring(0)
    partial_product(1)
    start_ring(1)
    partial_product(2)
    start_ring(2)

    high, low = split(pan2[...] * second_own)
    pan2_cat[:, 0:B] = high
    pan2_cat[:, B : 2 * B] = low

    def wide_product(there):
        at = pl.ds(pl.multiple_of(there * B, B), B)
        both = mul(inv_high[:, at], pan2_cat[...], ROWS)
        rest = mul(inv_low[:, at], pan2_cat[:, 0:B], ROWS)
        total = both[:, 0:B] + (both[:, B : 2 * B] + rest)
        wide[there] = total.reshape(4, 2, H, B)
        copies.send(("pairs", step), wide.at[there, :, 1 - core], wide_in.at[there], partner)

    def wide_ready(step):
        there = turn(x, step)
        copies.wait(("pairs", step), wide_in.at[there], partner)
        for lo in range(4):
            wide[there, lo, core] = wide[there, lo, core] + wide_in[there, lo]

    step = 2
    wide_product(turn(x, 2))
    ring[0].relay()
    step = 1
    wide_product(turn(x, 1))
    ring[1].relay()
    step = 3
    wide_product(turn(x, 3))
    ring[2].relay()

    def to_partner_half(chunk):
        quarter[chunk, 0], quarter[chunk, 1] = ring[chunk].finish()
        copies.send(("half", chunk), quarter.at[chunk], quarter_in.at[chunk], along_z(4))

    to_partner_half(0)
    step = 0
    wide_product(x)
    to_partner_half(1)
    to_partner_half(2)

    across = Scatter(
        copies, "wide", x, x_plus, x_minus,
        lambda q, h: wide.at[q, pl.ds(2 * h, 2), core],
        lambda h: wide_relay.at[h],
        lambda h: wide_direct.at[h],
        lambda h: wide_final.at[h],
    )
    wide_ready(2)
    across.start_far()
    wide_ready(1)
    across.start_plus()
    wide_ready(3)
    across.start_minus()
    wide_ready(0)

    turned_copies = []
    for step in range(1, 8):
        there = turn(row, step, 8)
        turned_copies.append(
            pltpu.make_async_remote_copy(
                src_ref=turned.at[there],
                dst_ref=turned_in,
                send_sem=send_sems.at[copies.slot(copies.sends, ("turned", step))],
                recv_sem=recv_sems.at[copies.slot(copies.recvs, "turned")],
                device_id=(there, col),
                device_id_type=MESH,
            )
        )

    @pl.when(is_owner)
    def _():
        block = pan1[pl.ds(pl.multiple_of(lax.rem(col, 4) * B, B), B), :]
        turned[...] = block.T.reshape(8, H, B)
        for copy in turned_copies:
            copy.start()
        turned_in[...] = turned[row]

    gather = []
    piece_copies = []
    for chunk in range(CH):
        gather.append(
            Gather(copies, ("gather", chunk), y, y_plus, y_minus, lambda q, h, chunk=chunk: column.at[chunk, q, h])
        )

    def give(chunk, half):
        remote = copies.make(
            ("piece", chunk), column.at[chunk, y, half], link_rows.at[chunk], taker(half), ("piece", chunk, half)
        )
        local = pltpu.make_async_copy(
            column.at[chunk, y, half],
            link_rows.at[chunk],
            recv_sems.at[copies.slot(copies.recvs, ("piece", chunk))],
        )
        here = is_self(half)
        piece_copies.append((half, remote))

        @pl.when(jnp.logical_and(gives, jnp.logical_not(here)))
        def _():
            remote.start()

        @pl.when(jnp.logical_and(gives, here))
        def _():
            local.start()

    for chunk in range(CH):
        copies.wait(("half", chunk), quarter_in.at[chunk], along_z(4))
        column[chunk, y] = quarter[chunk] + quarter_in[chunk]
        gather[chunk].start()
        give(chunk, 0)
        give(chunk, 1)

    across.relay()
    for chunk in range(CH):
        gather[chunk].relay()

    link_high[...], link_low[...] = split(link[...])
    base[...] = product(split(diag[...]), (link_high[...], link_low[...]))

    mine[0:2], mine[2:4] = across.finish()
    for step in range(1, 4):
        there = turn(zl, step)
        copies.send(("line", step), mine.at[there], mine_in.at[step - 1], device(zl=there))

    for chunk in range(CH):
        gather[chunk].near()
        gather[chunk].far()
        column_first[:, chunk * W : (chunk + 1) * W] = column[chunk].reshape(B, W)

    @pl.when(jnp.logical_not(is_owner))
    def _():
        turned_copies[0].wait_recv()

    whole = split(column_first[...])
    slice_first = product(split(turned_in[...]), whole)
    both = mul(whole[0], pan2_cat[...], ROWS)
    rest = mul(whole[1], pan2_cat[:, 0:B], ROWS)
    cross[...] = both[:, 0:B] + (both[:, B : 2 * B] + rest)
    pair[0] = slice_first.reshape(3, S, B)
    slice_second = cross[pl.ds(pl.multiple_of(row * H, H), H), :] - product(
        split(slice_first), (link_high[...], link_low[...])
    )
    pair[1] = slice_second.reshape(3, S, B)
    copies.send("pair", pair.at[1 - core], pair_in, partner)
    copies.wait("pair", pair_in, partner)
    slices[...] = pair[core] + pair_in[...]
    for step, there in ((1, x_plus), (2, x_far), (3, x_minus)):
        copies.send(("slice", step), slices.at[jnp.minimum(turn(x, step), 2)], slices_in.at[step - 1], there)
    for step, there in ((1, x_minus), (2, x_far), (3, x_plus)):
        copies.wait(("slice", step), slices_in.at[step - 1], there)
    depth[z] = (slices[jnp.minimum(x, 2)] + slices_in[0]) + (slices_in[1] + slices_in[2])
    for step in range(1, 8):
        copies.send(("depth", step), depth.at[z], depth.at[z], along_z(step))

    for step in range(1, 4):
        copies.wait(("line", step), mine_in.at[step - 1], device(zl=turn(zl, 4 - step)))
    for chunk in range(CH):
        copies.wait(("piece", chunk), link_rows.at[chunk], partner)
    block_row = row * 4 + lax.div(col, 8)
    rows_here = jnp.concatenate([link_rows[chunk] for chunk in range(CH)], axis=1)
    total = (mine[zl] + mine_in[0]) + (mine_in[1] + mine_in[2])
    total = total + product(split(rows_here), (link_high[...], link_low[...]))
    column_second[...] = total * (-marks[1, block_row].astype(F32))

    for step in range(1, 8):
        copies.wait(("depth", step), depth.at[turn(z, 8 - step, 8)], along_z(8 - step))
    for half in range(2):
        grid[core, y, half, x] = ((depth[4 * half] + depth[4 * half + 1]) + depth[4 * half + 2]) + depth[4 * half + 3]
    gather_x = Gather(copies, "gather_x", x, x_plus, x_minus, lambda q, h: grid.at[core, y, h, q])
    gather_x.start()
    gather_x.relay()
    gather_x.near()
    gather_x.far()
    gather_y = Gather(copies, "gather_y", y, y_plus, y_minus, lambda q, h: grid.at[core, q, h, pl.ds(0, 3)])
    gather_y.start()

    def pass_on(step):
        there = turn(y, step)
        copies.send(("swap", step), grid.at[core, there, :, pl.ds(0, 3)], grid.at[core, there, :, pl.ds(0, 3)], partner)

    pass_on(0)
    gather_y.relay()
    gather_y.near()
    pass_on(3)
    pass_on(1)
    gather_y.far()
    pass_on(2)
    for step in (0, 3, 1, 2):
        there = turn(y, step)
        copies.wait(("swap", step), grid.at[1 - core, there, :, pl.ds(0, 3)], partner)
    for high_z in range(2):
        for y_at in range(4):
            at = pl.ds((high_z * 4 + y_at) * H, H)
            diag_first[at, :] = diag[at, :] - grid[0, y_at, high_z, 0:3].reshape(H, B)
            corner[at, :] = -(base[at, :] + grid[1, y_at, high_z, 0:3].reshape(H, B))

    copies.finish()
    for half, copy in piece_copies:

        @pl.when(jnp.logical_and(gives, jnp.logical_not(is_self(half))))
        def _(copy=copy):
            copy.wait_send()

    @pl.when(is_owner)
    def _():
        for copy in turned_copies:
            copy.wait_send()


def body(inverse_blocks, panel_first, panel_second, panel_link, diag_inverse, ancestors):
    vmem = pl.BlockSpec(memory_space=pltpu.VMEM)
    shape = jax.ShapeDtypeStruct
    return pl.pallas_call(
        kernel,
        out_shape=(shape((B, B), F32), shape((B, B), F32), shape((H, B), F32), shape((B, B), F32)),
        in_specs=[pl.BlockSpec(memory_space=pltpu.SMEM)] + [vmem] * 5,
        out_specs=(vmem,) * 4,
        scratch_shapes=[
            pltpu.VMEM((B, 4 * B), BF16),
            pltpu.VMEM((B, 4 * B), BF16),
            pltpu.VMEM((CH, 4 * B, 2 * W), BF16),
            pltpu.VMEM((B, 2 * B), BF16),
            pltpu.VMEM((B, B), BF16),
            pltpu.VMEM((B, B), BF16),
            pltpu.VMEM((B, B), F32),
            pltpu.VMEM((CH, 4, 2, H, W), F32),
            pltpu.VMEM((CH, 2, H, W), F32),
            pltpu.VMEM((CH, 2, H, W), F32),
            pltpu.VMEM((CH, 2, H, W), F32),
            pltpu.VMEM((CH, 2, H, W), F32),
            pltpu.VMEM((CH, 2, H, W), F32),
            pltpu.VMEM((CH, 4, 2, H, W), F32),
            pltpu.VMEM((4, 4, 2, H, B), F32),
            pltpu.VMEM((4, 4, H, B), F32),
            pltpu.VMEM((2, 2, H, B), F32),
            pltpu.VMEM((2, 2, H, B), F32),
            pltpu.VMEM((2, 2, H, B), F32),
            pltpu.VMEM((4, H, B), F32),
            pltpu.VMEM((3, H, B), F32),
            pltpu.VMEM((CH, H, W), F32),
            pltpu.VMEM((8, H, B), F32),
            pltpu.VMEM((H, B), F32),
            pltpu.VMEM((B, B), F32),
            pltpu.VMEM((2, 3, S, B), F32),
            pltpu.VMEM((3, S, B), F32),
            pltpu.VMEM((3, S, B), F32),
            pltpu.VMEM((3, S, B), F32),
            pltpu.VMEM((8, S, B), F32),
            pltpu.VMEM((2, 4, 2, 4, S, B), F32),
            pltpu.SemaphoreType.DMA((112,)),
            pltpu.SemaphoreType.DMA((112,)),
        ],
        compiler_params=pltpu.CompilerParams(
            collective_id=0, has_side_effects=True, vmem_limit_bytes=60 * 1024 * 1024
        ),
    )(ancestors, inverse_blocks, panel_first, panel_second, panel_link, diag_inverse)


def solution(mesh):
    placed = (P("pcol", "prow"), P("prow", None), P("pcol", None), P(), P(), P())
    return jax.shard_map(
        body,
        mesh=mesh,
        in_specs=placed,
        out_specs=(P("pcol", None), P(), P(("prow", "pcol"), None), P()),
        check_vma=False,
    )
```

```python
import functools

import jax
import jax.numpy as jnp
from jax import lax
from jax.experimental import pallas as pl
from jax.experimental.pallas import tpu as pltpu
from jax.sharding import PartitionSpec as P

MESH = pl.DeviceIdType.MESH
F32 = jnp.float32
BF16 = jnp.bfloat16
B = 384
CH = 3
W = 128
H = 48
S = 16
ROWS = (((0,), (0,)), ((), ()))
PLAIN = (((1,), (0,)), ((), ()))


def split(value):
    high = value.astype(BF16)
    low = (value - high.astype(F32)).astype(BF16)
    return high, low


def mul(left, right, dims=PLAIN):
    return lax.dot_general(left, right, dims, preferred_element_type=F32)


def product(left, right, dims=PLAIN):
    left_high, left_low = left
    right_high, right_low = right
    return mul(left_high, right_high, dims) + (mul(left_high, right_low, dims) + mul(left_low, right_high, dims))


class Copies:
    def __init__(self, send_sems, recv_sems):
        self.send_sems, self.recv_sems = send_sems, recv_sems
        self.sends, self.recvs, self.sent = {}, {}, []

    def slot(self, table, key):
        if key not in table:
            table[key] = len(table)
        return table[key]

    def make(self, key, src, dst, device, send_key=None):
        send = self.slot(self.sends, key if send_key is None else send_key)
        recv = self.slot(self.recvs, key)
        return pltpu.make_async_remote_copy(
            src_ref=src,
            dst_ref=dst,
            send_sem=self.send_sems.at[send],
            recv_sem=self.recv_sems.at[recv],
            device_id=device,
            device_id_type=MESH,
        )

    def send(self, key, src, dst, device):
        copy = self.make(key, src, dst, device)
        copy.start()
        self.sent.append(copy)

    def wait(self, key, dst, device):
        self.make(key, dst, dst, device).wait_recv()

    def finish(self):
        for copy in self.sent:
            copy.wait_send()


class Ring:
    def __init__(self, copies, name, pos, plus, minus, get):
        self.copies, self.name, self.pos, self.plus, self.minus, self.get = copies, name, pos, plus, minus, get

    def at(self, offset, half):
        return self.get(lax.rem(self.pos + offset, 4), half)


class Scatter(Ring):
    def __init__(self, copies, name, pos, plus, minus, get, relay, direct, final):
        super().__init__(copies, name, pos, plus, minus, get)
        self.relayed, self.direct, self.final = relay, direct, final

    def start_far(self):
        self.copies.send((self.name, 0), self.at(2, 0), self.relayed(0), self.plus)
        self.copies.send((self.name, 1), self.at(2, 1), self.relayed(1), self.minus)

    def start_plus(self):
        self.copies.send((self.name, 2), self.at(1, 1), self.direct(0), self.plus)

    def start_minus(self):
        self.copies.send((self.name, 3), self.at(3, 0), self.direct(1), self.minus)

    def relay(self):
        self.copies.wait((self.name, 0), self.relayed(0), self.minus)
        mine = self.at(1, 0)
        mine[...] = mine[...] + self.relayed(0)[...]
        self.copies.send((self.name, 4), mine, self.final(0), self.plus)
        self.copies.wait((self.name, 1), self.relayed(1), self.plus)
        mine = self.at(3, 1)
        mine[...] = mine[...] + self.relayed(1)[...]
        self.copies.send((self.name, 5), mine, self.final(1), self.minus)

    def finish(self):
        self.copies.wait((self.name, 2), self.direct(0), self.minus)
        self.copies.wait((self.name, 3), self.direct(1), self.plus)
        self.copies.wait((self.name, 4), self.final(0), self.minus)
        self.copies.wait((self.name, 5), self.final(1), self.plus)
        first = self.at(0, 0)[...] + (self.direct(1)[...] + self.final(0)[...])
        second = self.at(0, 1)[...] + (self.direct(0)[...] + self.final(1)[...])
        return first, second


class Gather(Ring):
    def start(self):
        for number, half, device in ((0, 0, self.plus), (1, 1, self.minus), (2, 1, self.plus), (3, 0, self.minus)):
            self.copies.send((self.name, number), self.at(0, half), self.at(0, half), device)

    def relay(self):
        self.copies.wait((self.name, 0), self.at(3, 0), self.minus)
        self.copies.send((self.name, 4), self.at(3, 0), self.at(3, 0), self.plus)
        self.copies.wait((self.name, 1), self.at(1, 1), self.plus)
        self.copies.send((self.name, 5), self.at(1, 1), self.at(1, 1), self.minus)

    def near(self):
        self.copies.wait((self.name, 2), self.at(3, 1), self.minus)
        self.copies.wait((self.name, 3), self.at(1, 0), self.plus)

    def far(self):
        self.copies.wait((self.name, 4), self.at(2, 0), self.minus)
        self.copies.wait((self.name, 5), self.at(2, 1), self.plus)


def kernel(
    marks, inv_hbm, pan1_hbm, pan2_hbm, link_hbm, diag_hbm, column_first, diag_first, column_second, corner,
    inv, pan1, pan2, link, diag, load_sems, inv_high, inv_low, pan1_cat, pan2_cat, link_high, link_low, base,
    part, part_relay, part_direct, part_final, quarter, quarter_in, column,
    wide, wide_in, wide_relay, wide_direct, wide_final, mine, mine_in, link_rows,
    turned, turned_in, cross, pair, pair_in, slices, slices_in, depth, grid,
    send_sems, recv_sems,
):
    row, col = lax.axis_index("prow"), lax.axis_index("pcol")
    y, zh = lax.rem(row, 4), lax.div(row, 4)
    x, zl, core = lax.div(col, 8), lax.rem(lax.div(col, 2), 4), lax.rem(col, 2)
    z = zh * 4 + zl

    def device(y=y, zh=zh, x=x, zl=zl, core=core):
        return (zh * 4 + y, (x * 4 + zl) * 2 + core)

    def turn(value, step, size=4):
        return lax.rem(value + step, size)

    def along_z(step):
        there = turn(z, step, 8)
        return device(zh=lax.div(there, 4), zl=lax.rem(there, 4))

    loads = []
    for block in range(4):
        at = pl.ds(block * B, B)
        loads.append((pan1_hbm.at[at, :], pan1.at[at, :]))
        loads.append((inv_hbm.at[:, at], inv.at[:, at]))
    loads += [(pan2_hbm, pan2), (link_hbm, link), (diag_hbm, diag)]
    loads = [pltpu.make_async_copy(src, dst, load_sems.at[at]) for at, (src, dst) in enumerate(loads)]

    y_plus, y_minus = device(y=turn(y, 1)), device(y=turn(y, 3))
    x_plus, x_minus, x_far = device(x=turn(x, 1)), device(x=turn(x, 3)), device(x=turn(x, 2))
    partner = device(core=1 - core)
    owner_row = lax.div(col, 4)
    is_owner = row == owner_row
    owner_y, owner_zh = lax.rem(owner_row, 4), lax.div(owner_row, 4)
    is_source = y == owner_y
    is_deputy = jnp.logical_and(is_source, zh != owner_zh)

    gives = zh == lax.div(col, 16)

    def taker(half):
        return (owner_row, lax.rem(col, 4) * 8 + y * 2 + half)

    def is_self(half):
        there = taker(half)
        return jnp.logical_and(there[0] == row, there[1] == col)

    giver = (zh * 4 + lax.div(lax.rem(col, 8), 2), row * 4 + lax.div(col, 8))
    from_self = jnp.logical_and(giver[0] == row, giver[1] == col)

    barrier = pltpu.get_barrier_semaphore()

    def greet(there):
        pl.semaphore_signal(barrier, inc=1, device_id=there, device_id_type=MESH)

    for there in (y_plus, y_minus, x_plus, x_minus, x_far, partner):
        greet(there)
    for step in range(1, 8):
        greet(along_z(step))

    @pl.when(jnp.logical_not(from_self))
    def _():
        greet(giver)

    @pl.when(jnp.logical_not(is_source))
    def _():
        greet(device(y=owner_y))

    for load in loads:
        load.start()

    copies = Copies(send_sems, recv_sems)

    first_own = marks[0, col].astype(F32)
    second_own = marks[1, col].astype(F32)
    for block in range(4):
        at = pl.ds(block * B, B)
        loads[2 * block].wait()
        loads[2 * block + 1].wait()
        scaled = pan1[at, :] * marks[0, row * 4 + block].astype(F32)
        high, low = split(scaled)
        for chunk in range(CH):
            lanes = slice(chunk * W, (chunk + 1) * W)
            pan1_cat[chunk, at, 0:W] = high[:, lanes]
            pan1_cat[chunk, at, W : 2 * W] = low[:, lanes]
        inv_high[:, at], inv_low[:, at] = split(inv[:, at])

    ring = []
    for chunk in range(CH):
        ring.append(
            Scatter(
                copies, ("part", chunk), y, y_plus, y_minus,
                lambda q, h, chunk=chunk: part.at[chunk, q, h],
                lambda h, chunk=chunk: part_relay.at[chunk, h],
                lambda h, chunk=chunk: part_direct.at[chunk, h],
                lambda h, chunk=chunk: part_final.at[chunk, h],
            )
        )

    def partial_product(chunk):
        both = mul(inv_high[...], pan1_cat[chunk])
        rest = mul(inv_low[...], pan1_cat[chunk, :, 0:W])
        total = (both[:, 0:W] + (both[:, W : 2 * W] + rest)) * (-first_own)
        part[chunk] = total.reshape(4, 2, H, W)

    def start_ring(chunk):
        ring[chunk].start_far()
        ring[chunk].start_plus()
        ring[chunk].start_minus()

    partial_product(0)
    waits = 13 + jnp.where(is_source, 3, 0)
    for half in range(2):
        waits = waits + jnp.where(jnp.logical_and(gives, jnp.logical_not(is_self(half))), 1, 0)
    pl.semaphore_wait(barrier, waits)
    start_ring(0)
    partial_product(1)
    start_ring(1)
    partial_product(2)
    start_ring(2)

    turned_copies = []
    for step in range(1, 4):
        turned_copies.append(
            copies.make(
                "turned", turned.at[zh * 4 + turn(y, step)], turned_in, device(y=turn(y, step)), ("turned", step)
            )
        )
    far = turned.at[pl.ds(4 * (1 - zh), 4)]
    turned_far = copies.make("turned_far", far, far, along_z(4))

    def turned_out():
        for copy in turned_copies:
            copy.start()
        turned_in[...] = turned[row]

    @pl.when(is_owner)
    def _():
        block = pan1[pl.ds(pl.multiple_of(lax.rem(col, 4) * B, B), B), :]
        turned[...] = block.T.reshape(8, H, B)
        turned_far.start()

    loads[8].wait()
    high, low = split(pan2[...] * second_own)
    pan2_cat[:, 0:B] = high
    pan2_cat[:, B : 2 * B] = low

    def wide_product(there):
        at = pl.ds(pl.multiple_of(there * B, B), B)
        both = mul(inv_high[:, at], pan2_cat[...], ROWS)
        rest = mul(inv_low[:, at], pan2_cat[:, 0:B], ROWS)
        total = both[:, 0:B] + (both[:, B : 2 * B] + rest)
        wide[there] = total.reshape(4, 2, H, B)
        copies.send(("pairs", step), wide.at[there, :, 1 - core], wide_in.at[there], partner)

    def wide_ready(step):
        there = turn(x, step)
        copies.wait(("pairs", step), wide_in.at[there], partner)
        for lo in range(4):
            wide[there, lo, core] = wide[there, lo, core] + wide_in[there, lo]

    step = 2
    wide_product(turn(x, 2))
    ring[0].relay()
    step = 1
    wide_product(turn(x, 1))
    ring[1].relay()
    step = 3
    wide_product(turn(x, 3))
    ring[2].relay()

    @pl.when(is_owner)
    def _():
        turned_out()

    def to_partner_half(chunk):
        quarter[chunk, 0], quarter[chunk, 1] = ring[chunk].finish()
        copies.send(("half", chunk), quarter.at[chunk], quarter_in.at[chunk], along_z(4))

    to_partner_half(0)
    step = 0
    wide_product(x)
    to_partner_half(1)
    to_partner_half(2)

    across = Scatter(
        copies, "wide", x, x_plus, x_minus,
        lambda q, h: wide.at[q, pl.ds(2 * h, 2), core],
        lambda h: wide_relay.at[h],
        lambda h: wide_direct.at[h],
        lambda h: wide_final.at[h],
    )
    wide_ready(2)
    across.start_far()
    wide_ready(1)
    across.start_plus()
    wide_ready(3)
    across.start_minus()
    wide_ready(0)

    gather = []
    piece_copies = []
    for chunk in range(CH):
        gather.append(
            Gather(copies, ("gather", chunk), y, y_plus, y_minus, lambda q, h, chunk=chunk: column.at[chunk, q, h])
        )

    def give(chunk, half):
        remote = copies.make(
            ("piece", chunk), column.at[chunk, y, half], link_rows.at[chunk], taker(half), ("piece", chunk, half)
        )
        local = pltpu.make_async_copy(
            column.at[chunk, y, half],
            link_rows.at[chunk],
            recv_sems.at[copies.slot(copies.recvs, ("piece", chunk))],
        )
        here = is_self(half)
        piece_copies.append((half, remote))

        @pl.when(jnp.logical_and(gives, jnp.logical_not(here)))
        def _():
            remote.start()

        @pl.when(jnp.logical_and(gives, here))
        def _():
            local.start()

    for chunk in range(CH):
        copies.wait(("half", chunk), quarter_in.at[chunk], along_z(4))
        column[chunk, y] = quarter[chunk] + quarter_in[chunk]
        gather[chunk].start()

    @pl.when(is_deputy)
    def _():
        turned_far.wait_recv()
        turned_out()

    for chunk in range(CH):
        gather[chunk].relay()
        give(chunk, 0)
        give(chunk, 1)
    across.relay()

    loads[9].wait()
    loads[10].wait()

    link_high[...], link_low[...] = split(link[...])
    base[...] = product(split(diag[...]), (link_high[...], link_low[...]))

    for chunk in range(CH):
        gather[chunk].near()
        gather[chunk].far()
        column_first[:, chunk * W : (chunk + 1) * W] = column[chunk].reshape(B, W)

    @pl.when(jnp.logical_not(is_source))
    def _():
        turned_copies[0].wait_recv()

    whole = split(column_first[...])
    slice_first = product(split(turned_in[...]), whole)
    both = mul(whole[0], pan2_cat[...], ROWS)
    rest = mul(whole[1], pan2_cat[:, 0:B], ROWS)
    cross[...] = both[:, 0:B] + (both[:, B : 2 * B] + rest)
    pair[0] = slice_first.reshape(3, S, B)
    slice_second = cross[pl.ds(pl.multiple_of(row * H, H), H), :] - product(
        split(slice_first), (link_high[...], link_low[...])
    )
    pair[1] = slice_second.reshape(3, S, B)
    copies.send("pair", pair.at[1 - core], pair_in, partner)
    copies.wait("pair", pair_in, partner)
    slices[...] = pair[core] + pair_in[...]
    for step, there in ((1, x_plus), (2, x_far), (3, x_minus)):
        copies.send(("slice", step), slices.at[jnp.minimum(turn(x, step), 2)], slices_in.at[step - 1], there)
    for step, there in ((1, x_minus), (2, x_far), (3, x_plus)):
        copies.wait(("slice", step), slices_in.at[step - 1], there)
    depth[z] = (slices[jnp.minimum(x, 2)] + slices_in[0]) + (slices_in[1] + slices_in[2])
    for step in range(1, 8):
        copies.send(("depth", step), depth.at[z], depth.at[z], along_z(step))

    mine[0:2], mine[2:4] = across.finish()
    for step in range(1, 4):
        there = turn(zl, step)
        copies.send(("line", step), mine.at[there], mine_in.at[step - 1], device(zl=there))

    for step in range(1, 8):
        copies.wait(("depth", step), depth.at[turn(z, 8 - step, 8)], along_z(8 - step))
    for half in range(2):
        grid[core, y, half, x] = ((depth[4 * half] + depth[4 * half + 1]) + depth[4 * half + 2]) + depth[4 * half + 3]
    gather_x = Gather(copies, "gather_x", x, x_plus, x_minus, lambda q, h: grid.at[core, y, h, q])
    gather_x.start()
    gather_x.relay()
    gather_x.near()
    gather_x.far()
    gather_y = Gather(copies, "gather_y", y, y_plus, y_minus, lambda q, h: grid.at[core, q, h, pl.ds(0, 3)])
    gather_y.start()

    def pass_on(step):
        there = turn(y, step)
        copies.send(("swap", step), grid.at[core, there, :, pl.ds(0, 3)], grid.at[core, there, :, pl.ds(0, 3)], partner)

    pass_on(0)
    gather_y.relay()
    gather_y.near()
    pass_on(3)
    pass_on(1)
    gather_y.far()
    pass_on(2)
    for step in range(1, 4):
        copies.wait(("line", step), mine_in.at[step - 1], device(zl=turn(zl, 4 - step)))
    for chunk in range(CH):
        copies.wait(("piece", chunk), link_rows.at[chunk], partner)
    block_row = row * 4 + lax.div(col, 8)
    rows_here = jnp.concatenate([link_rows[chunk] for chunk in range(CH)], axis=1)
    total = (mine[zl] + mine_in[0]) + (mine_in[1] + mine_in[2])
    total = total + product(split(rows_here), (link_high[...], link_low[...]))
    column_second[...] = total * (-marks[1, block_row].astype(F32))

    for step in (0, 3, 1, 2):
        there = turn(y, step)
        copies.wait(("swap", step), grid.at[1 - core, there, :, pl.ds(0, 3)], partner)
    for high_z in range(2):
        for y_at in range(4):
            at = pl.ds((high_z * 4 + y_at) * H, H)
            diag_first[at, :] = diag[at, :] - grid[0, y_at, high_z, 0:3].reshape(H, B)
            corner[at, :] = -(base[at, :] + grid[1, y_at, high_z, 0:3].reshape(H, B))

    copies.finish()
    for half, copy in piece_copies:

        @pl.when(jnp.logical_and(gives, jnp.logical_not(is_self(half))))
        def _(copy=copy):
            copy.wait_send()

    @pl.when(is_source)
    def _():
        for copy in turned_copies:
            copy.wait_send()

    @pl.when(is_owner)
    def _():
        turned_far.wait_send()


def deliver(*refs):
    sems = refs[-1]
    moves = [pltpu.make_async_copy(refs[at], refs[4 + at], sems.at[at]) for at in range(4)]
    for move in moves:
        move.start()
    for move in moves:
        move.wait()


def body(*arrays):
    *arrays, ancestors = arrays
    vmem = pl.BlockSpec(memory_space=pltpu.VMEM)
    hbm = pl.BlockSpec(memory_space=pltpu.HBM)
    shape = jax.ShapeDtypeStruct
    sizes = ((B, B), (B, B), (H, B), (B, B))
    held = pl.pallas_call(
        kernel,
        out_shape=tuple(pltpu.VMEM(size, F32) for size in sizes),
        in_specs=[pl.BlockSpec(memory_space=pltpu.SMEM)] + [hbm] * 5,
        out_specs=(vmem,) * 4,
        scratch_shapes=[
            pltpu.VMEM((B, 4 * B), F32),
            pltpu.VMEM((4 * B, B), F32),
            pltpu.VMEM((B, B), F32),
            pltpu.VMEM((B, B), F32),
            pltpu.VMEM((B, B), F32),
            pltpu.SemaphoreType.DMA((11,)),
            pltpu.VMEM((B, 4 * B), BF16),
            pltpu.VMEM((B, 4 * B), BF16),
            pltpu.VMEM((CH, 4 * B, 2 * W), BF16),
            pltpu.VMEM((B, 2 * B), BF16),
            pltpu.VMEM((B, B), BF16),
            pltpu.VMEM((B, B), BF16),
            pltpu.VMEM((B, B), F32),
            pltpu.VMEM((CH, 4, 2, H, W), F32),
            pltpu.VMEM((CH, 2, H, W), F32),
            pltpu.VMEM((CH, 2, H, W), F32),
            pltpu.VMEM((CH, 2, H, W), F32),
            pltpu.VMEM((CH, 2, H, W), F32),
            pltpu.VMEM((CH, 2, H, W), F32),
            pltpu.VMEM((CH, 4, 2, H, W), F32),
            pltpu.VMEM((4, 4, 2, H, B), F32),
            pltpu.VMEM((4, 4, H, B), F32),
            pltpu.VMEM((2, 2, H, B), F32),
            pltpu.VMEM((2, 2, H, B), F32),
            pltpu.VMEM((2, 2, H, B), F32),
            pltpu.VMEM((4, H, B), F32),
            pltpu.VMEM((3, H, B), F32),
            pltpu.VMEM((CH, H, W), F32),
            pltpu.VMEM((8, H, B), F32),
            pltpu.VMEM((H, B), F32),
            pltpu.VMEM((B, B), F32),
            pltpu.VMEM((2, 3, S, B), F32),
            pltpu.VMEM((3, S, B), F32),
            pltpu.VMEM((3, S, B), F32),
            pltpu.VMEM((3, S, B), F32),
            pltpu.VMEM((8, S, B), F32),
            pltpu.VMEM((2, 4, 2, 4, S, B), F32),
            pltpu.SemaphoreType.DMA((112,)),
            pltpu.SemaphoreType.DMA((112,)),
        ],
        compiler_params=pltpu.CompilerParams(
            collective_id=0, has_side_effects=True, vmem_limit_bytes=44 * 1024 * 1024
        ),
    )(ancestors, *[pltpu.with_memory_space_constraint(given, pltpu.HBM) for given in arrays])
    held = [pltpu.with_memory_space_constraint(made, pltpu.VMEM) for made in held]
    return pl.pallas_call(
        deliver,
        out_shape=tuple(shape(size, F32) for size in sizes),
        in_specs=[vmem] * 4,
        out_specs=(hbm,) * 4,
        scratch_shapes=[pltpu.SemaphoreType.DMA((4,))],
    )(*held)


def solution(mesh):
    placed = (P("pcol", "prow"), P("prow", None), P("pcol", None), P(), P(), P())
    return jax.shard_map(
        body,
        mesh=mesh,
        in_specs=placed,
        out_specs=(P("pcol", None), P(), P(("prow", "pcol"), None), P()),
        check_vma=False,
    )
```

```python
import functools

import jax
import jax.numpy as jnp
from jax import lax
from jax.experimental import pallas as pl
from jax.experimental.pallas import tpu as pltpu
from jax.sharding import PartitionSpec as P

MESH = pl.DeviceIdType.MESH
F32 = jnp.float32
BF16 = jnp.bfloat16
B = 384
CH = 3
W = 128
H = 48
Q = 96
S = 16
ROWS = (((0,), (0,)), ((), ()))
PLAIN = (((1,), (0,)), ((), ()))


def split(value):
    high = value.astype(BF16)
    low = (value - high.astype(F32)).astype(BF16)
    return high, low


def mul(left, right, dims=PLAIN):
    return lax.dot_general(left, right, dims, preferred_element_type=F32)


def product(left, right, dims=PLAIN):
    left_high, left_low = left
    right_high, right_low = right
    return mul(left_high, right_high, dims) + (mul(left_high, right_low, dims) + mul(left_low, right_high, dims))


class Copies:
    def __init__(self, send_sems, recv_sems):
        self.send_sems, self.recv_sems = send_sems, recv_sems
        self.sends, self.recvs, self.sent = {}, {}, []

    def slot(self, table, key):
        if key not in table:
            table[key] = len(table)
        return table[key]

    def make(self, key, src, dst, device, send_key=None):
        send = self.slot(self.sends, key if send_key is None else send_key)
        recv = self.slot(self.recvs, key)
        return pltpu.make_async_remote_copy(
            src_ref=src,
            dst_ref=dst,
            send_sem=self.send_sems.at[send],
            recv_sem=self.recv_sems.at[recv],
            device_id=device,
            device_id_type=MESH,
        )

    def send(self, key, src, dst, device):
        copy = self.make(key, src, dst, device)
        copy.start()
        self.sent.append(copy)

    def wait(self, key, dst, device):
        self.make(key, dst, dst, device).wait_recv()

    def finish(self):
        for copy in self.sent:
            copy.wait_send()


class Exchange:
    def __init__(self, copies, name, pos, size, device, src, dst, land):
        self.copies, self.name, self.pos, self.size, self.device = copies, name, pos, size, device
        self.src, self.dst, self.land = src, dst, land
        self.steps = [2, 1, 3] if size == 4 else [4, 3, 5, 2, 6, 1, 7]

    def at(self, step):
        return lax.rem(self.pos + step, self.size)

    def start(self):
        for step in self.steps:
            there = self.at(step)
            self.copies.send((self.name, step), self.src(there), self.dst(step), self.device(there))

    def wait(self, step):
        back = self.at(self.size - step)
        self.copies.wait((self.name, step), self.land(step, back), self.device(back))

    def finish(self):
        for step in reversed(self.steps):
            self.wait(step)


def kernel(
    marks, inv_hbm, pan1_hbm, pan2_hbm, link_hbm, diag_hbm, column_first, diag_first, column_second, corner,
    inv, pan1, pan2, link, diag, load_sems, inv_high, inv_low, pan1_cat, pan2_cat, link_high, link_low,
    part, part_in, quarter, quarter_in, column,
    wide, wide_in, wide_far, mine, mine_in, link_rows,
    turned, turned_in, cross, pair, pair_in, slices, slices_in, depth, grid,
    send_sems, recv_sems,
):
    row, col = lax.axis_index("prow"), lax.axis_index("pcol")
    y, zh = lax.rem(row, 4), lax.div(row, 4)
    x, zl, core = lax.div(col, 8), lax.rem(lax.div(col, 2), 4), lax.rem(col, 2)
    z = zh * 4 + zl

    def device(y=y, zh=zh, x=x, zl=zl, core=core):
        return (zh * 4 + y, (x * 4 + zl) * 2 + core)

    def turn(value, step, size=4):
        return lax.rem(value + step, size)

    def at_z(there):
        return device(zh=lax.div(there, 4), zl=lax.rem(there, 4))

    def at_y(there):
        return device(y=there)

    def at_x(there):
        return device(x=there)

    loads = []
    for block in range(4):
        at = pl.ds(block * B, B)
        loads.append((pan1_hbm.at[at, :], pan1.at[at, :]))
        loads.append((inv_hbm.at[:, at], inv.at[:, at]))
    loads += [(pan2_hbm, pan2), (link_hbm, link), (diag_hbm, diag)]
    loads = [pltpu.make_async_copy(src, dst, load_sems.at[at]) for at, (src, dst) in enumerate(loads)]

    partner = device(core=1 - core)
    opposite = at_z(turn(z, 4, 8))
    owner_row = lax.div(col, 4)
    is_owner = row == owner_row
    owner_y, owner_zh = lax.rem(owner_row, 4), lax.div(owner_row, 4)
    is_source = y == owner_y
    is_deputy = jnp.logical_and(is_source, zh != owner_zh)

    gives = zh == lax.div(col, 16)

    def taker(half):
        return (owner_row, lax.rem(col, 4) * 8 + y * 2 + half)

    def is_self(half):
        there = taker(half)
        return jnp.logical_and(there[0] == row, there[1] == col)

    giver = (zh * 4 + lax.div(lax.rem(col, 8), 2), row * 4 + lax.div(col, 8))
    from_self = jnp.logical_and(giver[0] == row, giver[1] == col)

    barrier = pltpu.get_barrier_semaphore()

    def greet(there):
        pl.semaphore_signal(barrier, inc=1, device_id=there, device_id_type=MESH)

    for step in (1, 2, 3):
        greet(at_y(turn(y, step)))
        greet(at_x(turn(x, step)))
    greet(partner)
    for step in range(1, 8):
        greet(at_z(turn(z, step, 8)))

    @pl.when(jnp.logical_not(from_self))
    def _():
        greet(giver)

    @pl.when(jnp.logical_not(is_source))
    def _():
        greet(device(y=owner_y))

    for load in loads:
        load.start()

    copies = Copies(send_sems, recv_sems)

    first_own = marks[0, col].astype(F32)
    second_own = marks[1, col].astype(F32)
    for block in range(4):
        at = pl.ds(block * B, B)
        loads[2 * block].wait()
        scaled = pan1[at, :] * marks[0, row * 4 + block].astype(F32)
        high, low = split(scaled)
        for chunk in range(CH):
            lanes = slice(chunk * W, (chunk + 1) * W)
            pan1_cat[chunk, at, 0:W] = high[:, lanes]
            pan1_cat[chunk, at, W : 2 * W] = low[:, lanes]
        loads[2 * block + 1].wait()
        inv_high[:, at], inv_low[:, at] = split(inv[:, at])

    def partial_product(chunk):
        both = mul(inv_high[...], pan1_cat[chunk])
        rest = mul(inv_low[...], pan1_cat[chunk, :, 0:W])
        total = (both[:, 0:W] + (both[:, W : 2 * W] + rest)) * (-first_own)
        part[chunk] = total.reshape(4, Q, W)

    scatter, gather, along_x, along_z, gather_x, gather_y = [], [], [], [], [], []
    for chunk in range(CH):
        scatter.append(
            Exchange(
                copies, ("part", chunk), y, 4, at_y,
                lambda there, k=chunk: part.at[k, there],
                lambda step, k=chunk: part_in.at[k, step - 1],
                lambda step, back, k=chunk: part_in.at[k, step - 1],
            )
        )
        gather.append(
            Exchange(
                copies, ("column", chunk), y, 4, at_y,
                lambda there, k=chunk: column.at[k, y],
                lambda step, k=chunk: column.at[k, y],
                lambda step, back, k=chunk: column.at[k, back],
            )
        )
        along_x.append(
            Exchange(
                copies, ("slices", chunk), x, 4, at_x,
                lambda there, k=chunk: slices.at[k, jnp.minimum(there, 2)],
                lambda step, k=chunk: slices_in.at[k, step - 1],
                lambda step, back, k=chunk: slices_in.at[k, step - 1],
            )
        )
        along_z.append(
            Exchange(
                copies, ("depth", chunk), z, 8, at_z,
                lambda there, k=chunk: depth.at[k, z],
                lambda step, k=chunk: depth.at[k, z],
                lambda step, back, k=chunk: depth.at[k, back],
            )
        )
        gather_x.append(
            Exchange(
                copies, ("grid_x", chunk), x, 4, at_x,
                lambda there, k=chunk: grid.at[k, core, y, :, x],
                lambda step, k=chunk: grid.at[k, core, y, :, x],
                lambda step, back, k=chunk: grid.at[k, core, y, :, back],
            )
        )
        gather_y.append(
            Exchange(
                copies, ("grid_y", chunk), y, 4, at_y,
                lambda there, k=chunk: grid.at[k, core, y, :, pl.ds(0, 3)],
                lambda step, k=chunk: grid.at[k, core, y, :, pl.ds(0, 3)],
                lambda step, back, k=chunk: grid.at[k, core, back, :, pl.ds(0, 3)],
            )
        )
    across = Exchange(
        copies, "wide", x, 4, at_x,
        lambda there: wide.at[there, :, core],
        lambda step: wide_far.at[step - 1],
        lambda step, back: wide_far.at[step - 1],
    )
    line = Exchange(
        copies, "line", zl, 4, lambda there: device(zl=there),
        lambda there: mine.at[there],
        lambda step: mine_in.at[step - 1],
        lambda step, back: mine_in.at[step - 1],
    )

    turned_copies = []
    for step in range(1, 4):
        turned_copies.append(
            copies.make(
                "turned", turned.at[zh * 4 + turn(y, step)], turned_in, at_y(turn(y, step)), ("turned", step)
            )
        )
    far = turned.at[pl.ds(4 * (1 - zh), 4)]
    turned_far = copies.make("turned_far", far, far, opposite)

    def turned_out():
        for copy in turned_copies:
            copy.start()
        turned_in[...] = turned[row]

    partial_product(0)

    @pl.when(is_owner)
    def _():
        block = pan1[pl.ds(pl.multiple_of(lax.rem(col, 4) * B, B), B), :]
        turned[...] = block.T.reshape(8, H, B)

    waits = 14 + jnp.where(is_source, 3, 0)
    for half in range(2):
        waits = waits + jnp.where(jnp.logical_and(gives, jnp.logical_not(is_self(half))), 1, 0)
    pl.semaphore_wait(barrier, waits)
    scatter[0].start()

    @pl.when(is_owner)
    def _():
        turned_far.start()

    partial_product(1)
    scatter[1].start()
    partial_product(2)
    scatter[2].start()

    loads[8].wait()
    high, low = split(pan2[...] * second_own)
    pan2_cat[:, 0:B] = high
    pan2_cat[:, B : 2 * B] = low

    def wide_product(step):
        there = turn(x, step)
        at = pl.ds(pl.multiple_of(there * B, B), B)
        both = mul(inv_high[:, at], pan2_cat[...], ROWS)
        rest = mul(inv_low[:, at], pan2_cat[:, 0:B], ROWS)
        total = both[:, 0:B] + (both[:, B : 2 * B] + rest)
        wide[there] = total.reshape(4, 2, H, B)
        copies.send(("pairs", step), wide.at[there, :, 1 - core], wide_in.at[there], partner)

    def wide_ready(step):
        there = turn(x, step)
        copies.wait(("pairs", step), wide_in.at[there], partner)
        for lo in range(4):
            wide[there, lo, core] = wide[there, lo, core] + wide_in[there, lo]

    def to_opposite(chunk):
        scatter[chunk].finish()
        quarter[chunk] = (part[chunk, y] + part_in[chunk, 0]) + (part_in[chunk, 1] + part_in[chunk, 2])
        copies.send(("half", chunk), quarter.at[chunk], quarter_in.at[chunk], opposite)

    wide_product(2)
    wide_product(1)
    to_opposite(0)

    @pl.when(is_owner)
    def _():
        turned_out()

    wide_product(3)
    to_opposite(1)
    wide_product(0)
    to_opposite(2)
    for step in (2, 1, 3):
        wide_ready(step)
        there = turn(x, step)
        copies.send(("wide", step), wide.at[there, :, core], wide_far.at[step - 1], at_x(there))
    wide_ready(0)

    @pl.when(is_deputy)
    def _():
        turned_far.wait_recv()
        turned_out()

    loads[9].wait()
    loads[10].wait()
    link_high[...], link_low[...] = split(link[...])

    for chunk in range(CH):
        copies.wait(("half", chunk), quarter_in.at[chunk], opposite)
        column[chunk, y] = quarter[chunk] + quarter_in[chunk]
        gather[chunk].start()

    piece_copies = []

    def give(chunk, half):
        src = column.at[chunk, y, pl.ds(half * H, H)]
        remote = copies.make(("piece", chunk), src, link_rows.at[chunk], taker(half), ("piece", chunk, half))
        local = pltpu.make_async_copy(src, link_rows.at[chunk], recv_sems.at[copies.slot(copies.recvs, ("piece", chunk))])
        here = is_self(half)
        piece_copies.append((half, remote))

        @pl.when(jnp.logical_and(gives, jnp.logical_not(here)))
        def _():
            remote.start()

        @pl.when(jnp.logical_and(gives, here))
        def _():
            local.start()

    for chunk in range(CH):
        give(chunk, 0)
        give(chunk, 1)

    @pl.when(jnp.logical_not(is_source))
    def _():
        turned_copies[0].wait_recv()

    turned_high, turned_low = split(turned_in[...])

    for chunk in range(CH):
        gather[chunk].finish()
        whole = column[chunk].reshape(B, W)
        column_first[:, chunk * W : (chunk + 1) * W] = whole
        whole = split(whole)
        slice_first = product((turned_high, turned_low), whole)
        both = mul(whole[0], pan2_cat[...], ROWS)
        rest = mul(whole[1], pan2_cat[:, 0:B], ROWS)
        cross[...] = both[:, 0:B] + (both[:, B : 2 * B] + rest)
        pair[chunk, 0] = slice_first.reshape(3, S, W)
        for third in range(3):
            pair[chunk, 1, third] = cross[pl.ds(pl.multiple_of(row * S, S), S), third * W : (third + 1) * W]
        copies.send(("pair", chunk), pair.at[chunk, 1 - core], pair_in.at[chunk], partner)
    for chunk in range(CH):
        copies.wait(("pair", chunk), pair_in.at[chunk], partner)
        slices[chunk] = pair[chunk, core] + pair_in[chunk]
        along_x[chunk].start()
    for chunk in range(CH):
        along_x[chunk].finish()
        depth[chunk, z] = (slices[chunk, jnp.minimum(x, 2)] + slices_in[chunk, 0]) + (
            slices_in[chunk, 1] + slices_in[chunk, 2]
        )
        along_z[chunk].start()

    across.finish()
    mine[...] = (wide[x, :, core] + wide_far[0]) + (wide_far[1] + wide_far[2])
    line.start()

    for chunk in range(CH):
        along_z[chunk].finish()
        for half in range(2):
            grid[chunk, core, y, half, x] = (
                (depth[chunk, 4 * half] + depth[chunk, 4 * half + 1]) + depth[chunk, 4 * half + 2]
            ) + depth[chunk, 4 * half + 3]
        gather_x[chunk].start()

    def pass_on(chunk, step):
        part_at = grid.at[chunk, core, turn(y, step), :, pl.ds(0, 3)]
        copies.send(("swap", chunk, step), part_at, part_at, partner)

    for chunk in range(CH):
        gather_x[chunk].finish()
        gather_y[chunk].start()
        pass_on(chunk, 0)
    for chunk in range(CH):
        for step in (1, 3, 2):
            gather_y[chunk].wait(step)
            pass_on(chunk, 4 - step)

    line.finish()
    for chunk in range(CH):
        copies.wait(("piece", chunk), link_rows.at[chunk], partner)
    block_row = row * 4 + lax.div(col, 8)
    rows_here = jnp.concatenate([link_rows[chunk] for chunk in range(CH)], axis=1)
    total = (mine[zl] + mine_in[0]) + (mine_in[1] + mine_in[2])
    total = total + product(split(rows_here), (link_high[...], link_low[...]))
    column_second[...] = total * (-marks[1, block_row].astype(F32))

    linked = []
    for chunk in range(CH):
        for step in (0, 3, 1, 2):
            part_at = grid.at[chunk, 1 - core, turn(y, step), :, pl.ds(0, 3)]
            copies.wait(("swap", chunk, step), part_at, partner)
        lanes = slice(chunk * W, (chunk + 1) * W)
        for piece in range(8):
            at = slice(piece * H, (piece + 1) * H)
            found = grid[chunk, 0, piece % 4, piece // 4, 0:3].reshape(H, W)
            diag_first[at, lanes] = diag[at, lanes] - found
        ready = split(diag_first[:, lanes])
        linked.append(product(ready, (link_high[lanes, :], link_low[lanes, :])))
    total = linked[0] + (linked[1] + linked[2])
    for chunk in range(CH):
        for piece in range(8):
            at = slice(chunk * W + piece * S, chunk * W + (piece + 1) * S)
            for third in range(3):
                lanes = slice(third * W, (third + 1) * W)
                corner[at, lanes] = -(total[at, lanes] + grid[chunk, 1, piece % 4, piece // 4, third])

    copies.finish()
    for half, copy in piece_copies:

        @pl.when(jnp.logical_and(gives, jnp.logical_not(is_self(half))))
        def _(copy=copy):
            copy.wait_send()

    @pl.when(is_source)
    def _():
        for copy in turned_copies:
            copy.wait_send()

    @pl.when(is_owner)
    def _():
        turned_far.wait_send()


def deliver(*refs):
    sems = refs[-1]
    moves = [pltpu.make_async_copy(refs[at], refs[4 + at], sems.at[at]) for at in range(4)]
    for move in moves:
        move.start()
    for move in moves:
        move.wait()


def body(*arrays):
    *arrays, ancestors = arrays
    vmem = pl.BlockSpec(memory_space=pltpu.VMEM)
    hbm = pl.BlockSpec(memory_space=pltpu.HBM)
    shape = jax.ShapeDtypeStruct
    sizes = ((B, B), (B, B), (H, B), (B, B))
    held = pl.pallas_call(
        kernel,
        out_shape=tuple(pltpu.VMEM(size, F32) for size in sizes),
        in_specs=[pl.BlockSpec(memory_space=pltpu.SMEM)] + [hbm] * 5,
        out_specs=(vmem,) * 4,
        scratch_shapes=[
            pltpu.VMEM((B, 4 * B), F32),
            pltpu.VMEM((4 * B, B), F32),
            pltpu.VMEM((B, B), F32),
            pltpu.VMEM((B, B), F32),
            pltpu.VMEM((B, B), F32),
            pltpu.SemaphoreType.DMA((11,)),
            pltpu.VMEM((B, 4 * B), BF16),
            pltpu.VMEM((B, 4 * B), BF16),
            pltpu.VMEM((CH, 4 * B, 2 * W), BF16),
            pltpu.VMEM((B, 2 * B), BF16),
            pltpu.VMEM((B, B), BF16),
            pltpu.VMEM((B, B), BF16),
            pltpu.VMEM((CH, 4, Q, W), F32),
            pltpu.VMEM((CH, 3, Q, W), F32),
            pltpu.VMEM((CH, Q, W), F32),
            pltpu.VMEM((CH, Q, W), F32),
            pltpu.VMEM((CH, 4, Q, W), F32),
            pltpu.VMEM((4, 4, 2, H, B), F32),
            pltpu.VMEM((4, 4, H, B), F32),
            pltpu.VMEM((3, 4, H, B), F32),
            pltpu.VMEM((4, H, B), F32),
            pltpu.VMEM((3, H, B), F32),
            pltpu.VMEM((CH, H, W), F32),
            pltpu.VMEM((8, H, B), F32),
            pltpu.VMEM((H, B), F32),
            pltpu.VMEM((W, B), F32),
            pltpu.VMEM((CH, 2, 3, S, W), F32),
            pltpu.VMEM((CH, 3, S, W), F32),
            pltpu.VMEM((CH, 3, S, W), F32),
            pltpu.VMEM((CH, 3, S, W), F32),
            pltpu.VMEM((CH, 8, S, W), F32),
            pltpu.VMEM((CH, 2, 4, 2, 4, S, W), F32),
            pltpu.SemaphoreType.DMA((112,)),
            pltpu.SemaphoreType.DMA((112,)),
        ],
        compiler_params=pltpu.CompilerParams(
            collective_id=0, has_side_effects=True, vmem_limit_bytes=44 * 1024 * 1024
        ),
    )(ancestors, *[pltpu.with_memory_space_constraint(given, pltpu.HBM) for given in arrays])
    held = [pltpu.with_memory_space_constraint(made, pltpu.VMEM) for made in held]
    return pl.pallas_call(
        deliver,
        out_shape=tuple(shape(size, F32) for size in sizes),
        in_specs=[vmem] * 4,
        out_specs=(hbm,) * 4,
        scratch_shapes=[pltpu.SemaphoreType.DMA((4,))],
    )(*held)


def solution(mesh):
    placed = (P("pcol", "prow"), P("prow", None), P("pcol", None), P(), P(), P())
    return jax.shard_map(
        body,
        mesh=mesh,
        in_specs=placed,
        out_specs=(P("pcol", None), P(), P(("prow", "pcol"), None), P()),
        check_vma=False,
    )
```

```python
import functools

import jax
import jax.numpy as jnp
from jax import lax
from jax.experimental import pallas as pl
from jax.experimental.pallas import tpu as pltpu
from jax.sharding import PartitionSpec as P

MESH = pl.DeviceIdType.MESH
F32 = jnp.float32
BF16 = jnp.bfloat16
B = 384
CH = 3
W = 128
H = 48
S = 16
SENDS = 14
RECVS = 40
ROWS = (((0,), (0,)), ((), ()))
PLAIN = (((1,), (0,)), ((), ()))


def split(value):
    high = value.astype(BF16)
    low = (value - high.astype(F32)).astype(BF16)
    return high, low


def mul(left, right, dims=PLAIN):
    return lax.dot_general(left, right, dims, preferred_element_type=F32)


def product(left, right, dims=PLAIN):
    left_high, left_low = left
    right_high, right_low = right
    return mul(left_high, right_high, dims) + (mul(left_high, right_low, dims) + mul(left_low, right_high, dims))


class Copies:
    def __init__(self, send_sems, recv_sems):
        self.send_sems, self.recv_sems = send_sems, recv_sems
        self.kinds, self.keys = {}, {}

    def recv_sem(self, key):
        return self.recv_sems.at[self.keys.setdefault(key, len(self.keys))]

    def make(self, key, src, dst, device):
        return pltpu.make_async_remote_copy(
            src_ref=src,
            dst_ref=dst,
            send_sem=self.send_sems.at[self.kinds.setdefault(key[0], len(self.kinds))],
            recv_sem=self.recv_sem(key),
            device_id=device,
            device_id_type=MESH,
        )

    def send(self, key, src, dst, device):
        self.make(key, src, dst, device).start()

    def wait(self, key, every, device):
        self.make(key, every, every, device).wait_recv()

    def sent(self, kind, every, device):
        self.make((kind, 0), every, every, device).wait_send()


class Ring:
    def __init__(self, copies, name, pos, plus, minus, get):
        self.copies, self.name, self.pos, self.plus, self.minus, self.get = copies, name, pos, plus, minus, get

    def at(self, offset, half):
        return self.get(lax.rem(self.pos + offset, 4), half)


class Scatter(Ring):
    def __init__(self, copies, name, pos, plus, minus, get, relay, direct, final):
        super().__init__(copies, name, pos, plus, minus, get)
        self.relayed, self.direct, self.final = relay, direct, final

    def start(self):
        self.start_far()
        self.start_plus()
        self.start_minus()

    def start_far(self):
        self.copies.send((self.name, 0), self.at(2, 0), self.relayed(0), self.plus)
        self.copies.send((self.name, 1), self.at(2, 1), self.relayed(1), self.minus)

    def start_plus(self):
        self.copies.send((self.name, 2), self.at(1, 1), self.direct(0), self.plus)

    def start_minus(self):
        self.copies.send((self.name, 3), self.at(3, 0), self.direct(1), self.minus)

    def relay(self):
        self.copies.wait((self.name, 0), self.relayed(0), self.minus)
        mine = self.at(1, 0)
        mine[...] = mine[...] + self.relayed(0)[...]
        self.copies.send((self.name, 4), mine, self.final(0), self.plus)
        self.copies.wait((self.name, 1), self.relayed(1), self.plus)
        mine = self.at(3, 1)
        mine[...] = mine[...] + self.relayed(1)[...]
        self.copies.send((self.name, 5), mine, self.final(1), self.minus)

    def finish(self):
        self.copies.wait((self.name, 2), self.direct(0), self.minus)
        self.copies.wait((self.name, 3), self.direct(1), self.plus)
        self.copies.wait((self.name, 4), self.final(0), self.minus)
        self.copies.wait((self.name, 5), self.final(1), self.plus)
        first = self.at(0, 0)[...] + (self.direct(1)[...] + self.final(0)[...])
        second = self.at(0, 1)[...] + (self.direct(0)[...] + self.final(1)[...])
        return first, second


class Exchange:
    def __init__(self, copies, key, pos, size, device, src, dst, every):
        self.copies, self.key, self.pos, self.size, self.device = copies, key, pos, size, device
        self.src, self.dst, self.every = src, dst, every
        self.steps = [2, 1, 3] if size == 4 else [4, 3, 5, 2, 6, 1, 7]

    def start(self):
        for step in self.steps:
            there = lax.rem(self.pos + step, self.size)
            self.copies.send(self.key, self.src(there), self.dst(step), self.device(there))

    def finish(self):
        self.copies.wait(self.key, self.every, self.device(lax.rem(self.pos + 1, self.size)))


def kernel(
    marks_hbm, inv_hbm, pan1_hbm, pan2_hbm, link_hbm, diag_hbm, column_first, diag_first, column_second, corner,
    marks, inv, pan1, pan2, link, diag, load_sems, inv_high, inv_low, pan1_cat, pan2_cat, link_high, link_low,
    part, part_in, quarter, quarter_in, column,
    wide, wide_in, wide_relay, wide_direct, wide_final, mine, mine_in, link_rows,
    turned, turned_in, cross, pair, pair_in, slices, slices_in, depth, grid,
    send_sems, recv_sems,
):
    row, col = lax.axis_index("prow"), lax.axis_index("pcol")
    y, zh = lax.rem(row, 4), lax.div(row, 4)
    x, zl, core = lax.div(col, 8), lax.rem(lax.div(col, 2), 4), lax.rem(col, 2)
    z = zh * 4 + zl

    def device(y=y, zh=zh, x=x, zl=zl, core=core):
        return (zh * 4 + y, (x * 4 + zl) * 2 + core)

    def turn(value, step, size=4):
        return lax.rem(value + step, size)

    def at_z(there):
        return device(zh=lax.div(there, 4), zl=lax.rem(there, 4))

    def at_y(there):
        return device(y=there)

    def at_x(there):
        return device(x=there)

    y_plus, y_minus = device(y=turn(y, 1)), device(y=turn(y, 3))
    x_plus, x_minus = device(x=turn(x, 1)), device(x=turn(x, 3))

    loads = []
    for block in range(4):
        at = pl.ds(block * B, B)
        loads.append((pan1_hbm.at[at, :], pan1.at[at, :]))
        loads.append((inv_hbm.at[:, at], inv.at[:, at]))
    loads += [(pan2_hbm, pan2), (link_hbm, link), (diag_hbm, diag), (marks_hbm, marks)]
    loads = [pltpu.make_async_copy(src, dst, load_sems.at[at]) for at, (src, dst) in enumerate(loads)]

    partner = device(core=1 - core)
    opposite = at_z(turn(z, 4, 8))
    after = (lax.div(col, 4), lax.rem(col, 4) * 8 + row)
    before = (lax.rem(col, 8), row * 4 + lax.div(col, 8))
    fixed = jnp.logical_and(after[0] == row, after[1] == col)
    moved = jnp.logical_not(fixed)

    barrier = pltpu.get_barrier_semaphore()

    def greet(there):
        pl.semaphore_signal(barrier, inc=1, device_id=there, device_id_type=MESH)

    loads[11].start()
    for step in (1, 2, 3):
        greet(at_y(turn(y, step)))
        greet(at_x(turn(x, step)))
    greet(partner)
    for step in range(1, 8):
        greet(at_z(turn(z, step, 8)))

    @pl.when(moved)
    def _():
        greet(after)
        greet(before)

    for load in loads[:11]:
        load.start()

    copies = Copies(send_sems, recv_sems)

    loads[11].wait()
    first_own = marks[0, col].astype(F32)
    second_own = marks[1, col].astype(F32)
    for block in range(4):
        at = pl.ds(block * B, B)
        loads[2 * block].wait()
        scaled = pan1[at, :] * marks[0, row * 4 + block].astype(F32)
        high, low = split(scaled)
        for chunk in range(CH):
            lanes = slice(chunk * W, (chunk + 1) * W)
            pan1_cat[chunk, at, 0:W] = high[:, lanes]
            pan1_cat[chunk, at, W : 2 * W] = low[:, lanes]
        loads[2 * block + 1].wait()
        inv_high[:, at], inv_low[:, at] = split(inv[:, at])

    def partial_product(chunk):
        both = mul(inv_high[...], pan1_cat[chunk])
        rest = mul(inv_low[...], pan1_cat[chunk, :, 0:W])
        total = (both[:, 0:W] + (both[:, W : 2 * W] + rest)) * (-first_own)
        part[chunk] = total.reshape(4, 2, H, W)

    scatter, gather, along_x, along_z, gather_x, gather_y = [], [], [], [], [], []
    for chunk in range(CH):
        scatter.append(
            Exchange(
                copies, ("part", chunk), y, 4, at_y,
                lambda there, k=chunk: part.at[k, there],
                lambda step, k=chunk: part_in.at[k, step - 1],
                part_in.at[chunk],
            )
        )
        gather.append(
            Exchange(
                copies, ("column", chunk), y, 4, at_y,
                lambda there, k=chunk: column.at[k, y],
                lambda step, k=chunk: column.at[k, y],
                column.at[chunk, pl.ds(0, 3)],
            )
        )
        along_x.append(
            Exchange(
                copies, ("slices", chunk), x, 4, at_x,
                lambda there, k=chunk: slices.at[k, jnp.minimum(there, 2)],
                lambda step, k=chunk: slices_in.at[k, step - 1],
                slices_in.at[chunk],
            )
        )
        along_z.append(
            Exchange(
                copies, ("depth", chunk), z, 8, at_z,
                lambda there, k=chunk: depth.at[k, z],
                lambda step, k=chunk: depth.at[k, z],
                depth.at[chunk, pl.ds(0, 7)],
            )
        )
        gather_x.append(
            Exchange(
                copies, ("grid_x", chunk), x, 4, at_x,
                lambda there, k=chunk: grid.at[k, core, y, :, x],
                lambda step, k=chunk: grid.at[k, core, y, :, x],
                grid.at[chunk, core, pl.ds(0, 3), :, 0],
            )
        )
        gather_y.append(
            Exchange(
                copies, ("grid_y", chunk), y, 4, at_y,
                lambda there, k=chunk: grid.at[k, core, y, :, pl.ds(0, 3)],
                lambda step, k=chunk: grid.at[k, core, y, :, pl.ds(0, 3)],
                grid.at[chunk, core, pl.ds(0, 3), :, pl.ds(0, 3)],
            )
        )
    across = Scatter(
        copies, "wide", x, x_plus, x_minus,
        lambda q, h: wide.at[q, pl.ds(2 * h, 2), core],
        lambda h: wide_relay.at[h],
        lambda h: wide_direct.at[h],
        lambda h: wide_final.at[h],
    )
    line = Exchange(
        copies, ("line", 0), zl, 4, lambda there: device(zl=there),
        lambda there: mine.at[there],
        lambda step: mine_in.at[step - 1],
        mine_in,
    )

    def permute(key, src, dst, there):
        remote = copies.make(key, src, dst, there)
        local = pltpu.make_async_copy(src, dst, copies.recv_sem(key))

        @pl.when(moved)
        def _():
            remote.start()

        @pl.when(fixed)
        def _():
            local.start()

    partial_product(0)

    block = pan1[pl.ds(pl.multiple_of(lax.div(col, 8) * B, B), B), :]
    turned[...] = block.T.reshape(8, H, B)
    pl.semaphore_wait(barrier, 14 + jnp.where(moved, 2, 0))
    scatter[0].start()

    partial_product(1)
    scatter[1].start()
    partial_product(2)
    scatter[2].start()

    loads[8].wait()
    high, low = split(pan2[...] * second_own)
    pan2_cat[:, 0:B] = high
    pan2_cat[:, B : 2 * B] = low

    def wide_product(step):
        there = turn(x, step)
        at = pl.ds(pl.multiple_of(there * B, B), B)
        both = mul(inv_high[:, at], pan2_cat[...], ROWS)
        rest = mul(inv_low[:, at], pan2_cat[:, 0:B], ROWS)
        total = both[:, 0:B] + (both[:, B : 2 * B] + rest)
        wide[there] = total.reshape(4, 2, H, B)
        copies.send(("pairs", step), wide.at[there, :, 1 - core], wide_in.at[there], partner)

    def wide_ready(step):
        there = turn(x, step)
        copies.wait(("pairs", step), wide_in.at[there], partner)
        for lo in range(4):
            wide[there, lo, core] = wide[there, lo, core] + wide_in[there, lo]

    def to_opposite(chunk):
        scatter[chunk].finish()
        quarter[chunk] = (part[chunk, y] + part_in[chunk, 0]) + (part_in[chunk, 1] + part_in[chunk, 2])
        copies.send(("half", chunk), quarter.at[chunk], quarter_in.at[chunk], opposite)

    wide_product(2)
    wide_product(1)
    to_opposite(0)
    wide_product(3)
    to_opposite(1)
    wide_product(0)
    to_opposite(2)
    permute(("turned", 0), turned.at[lax.rem(col, 8)], turned_in, before)
    wide_ready(2)
    across.start_far()
    wide_ready(1)
    across.start_plus()
    wide_ready(3)
    across.start_minus()
    wide_ready(0)
    loads[9].wait()
    loads[10].wait()
    link_high[...], link_low[...] = split(link[...])
    for chunk in range(CH):
        copies.wait(("half", chunk), quarter_in.at[chunk], opposite)
        column[chunk, y] = quarter[chunk] + quarter_in[chunk]
        gather[chunk].start()

    across.relay()

    copies.wait(("turned", 0), turned_in, partner)
    turned_high, turned_low = split(turned_in[...])

    for chunk in range(CH):
        gather[chunk].finish()
        whole = column[chunk].reshape(B, W)
        column_first[:, chunk * W : (chunk + 1) * W] = whole
        whole = split(whole)
        slice_first = product((turned_high, turned_low), whole)
        both = mul(whole[0], pan2_cat[...], ROWS)
        rest = mul(whole[1], pan2_cat[:, 0:B], ROWS)
        cross[...] = both[:, 0:B] + (both[:, B : 2 * B] + rest)
        pair[chunk, 0] = slice_first.reshape(3, S, W)
        for third in range(3):
            pair[chunk, 1, third] = cross[pl.ds(pl.multiple_of(row * S, S), S), third * W : (third + 1) * W]
        copies.send(("pair", chunk), pair.at[chunk, 1 - core], pair_in.at[chunk], partner)
    for chunk in range(CH):
        copies.wait(("pair", chunk), pair_in.at[chunk], partner)
        slices[chunk] = pair[chunk, core] + pair_in[chunk]
        along_x[chunk].start()
    for chunk in range(CH):
        along_x[chunk].finish()
        depth[chunk, z] = (slices[chunk, jnp.minimum(x, 2)] + slices_in[chunk, 0]) + (
            slices_in[chunk, 1] + slices_in[chunk, 2]
        )
        along_z[chunk].start()

    permute(("rows", 0), column.at[:, lax.div(row, 2), lax.rem(row, 2)], link_rows, after)

    for chunk in range(CH):
        along_z[chunk].finish()
        for half in range(2):
            grid[chunk, core, y, half, x] = (
                (depth[chunk, 4 * half] + depth[chunk, 4 * half + 1]) + depth[chunk, 4 * half + 2]
            ) + depth[chunk, 4 * half + 3]
        gather_x[chunk].start()

    mine[0:2], mine[2:4] = across.finish()
    line.start()

    def pass_on(chunk, step):
        part_at = grid.at[chunk, core, turn(y, step), :, pl.ds(0, 3)]
        copies.send(("swap", chunk), part_at, part_at, partner)

    for chunk in range(CH):
        gather_x[chunk].finish()
        gather_y[chunk].start()
        pass_on(chunk, 0)
    for chunk in range(CH):
        gather_y[chunk].finish()
        for step in (1, 3, 2):
            pass_on(chunk, step)

    line.finish()
    copies.wait(("rows", 0), link_rows, partner)
    block_row = row * 4 + lax.div(col, 8)
    rows_here = jnp.concatenate([link_rows[chunk] for chunk in range(CH)], axis=1)
    total = (mine[zl] + mine_in[0]) + (mine_in[1] + mine_in[2])
    total = total + product(split(rows_here), (link_high[...], link_low[...]))
    column_second[...] = total * (-marks[1, block_row].astype(F32))

    linked = []
    for chunk in range(CH):
        copies.wait(("swap", chunk), grid.at[chunk, 1 - core, :, :, pl.ds(0, 3)], partner)
        lanes = slice(chunk * W, (chunk + 1) * W)
        for piece in range(8):
            at = slice(piece * H, (piece + 1) * H)
            found = grid[chunk, 0, piece % 4, piece // 4, 0:3].reshape(H, W)
            diag_first[at, lanes] = diag[at, lanes] - found
        ready = split(diag_first[:, lanes])
        linked.append(product(ready, (link_high[lanes, :], link_low[lanes, :])))
    total = linked[0] + (linked[1] + linked[2])
    for chunk in range(CH):
        for piece in range(8):
            at = slice(chunk * W + piece * S, chunk * W + (piece + 1) * S)
            for third in range(3):
                lanes = slice(third * W, (third + 1) * W)
                corner[at, lanes] = -(total[at, lanes] + grid[chunk, 1, piece % 4, piece // 4, third])

    for kind, every in (
        ("part", part.at[:, pl.ds(0, 3)]),
        ("half", quarter),
        ("column", column.at[:, pl.ds(0, 3)]),
        ("pairs", wide_in),
        ("wide", wide.at[pl.ds(0, 3), :, 0]),
        ("line", mine_in),
        ("pair", pair_in),
        ("slices", slices_in),
        ("depth", depth.at[:, pl.ds(0, 7)]),
        ("grid_x", grid.at[:, 0, pl.ds(0, 3), :, 0]),
        ("grid_y", grid.at[:, 0, pl.ds(0, 3), :, pl.ds(0, 3)]),
        ("swap", grid.at[:, 0, :, :, pl.ds(0, 3)]),
    ):
        copies.sent(kind, every, partner)

    @pl.when(moved)
    def _():
        copies.sent("turned", turned_in, partner)
        copies.sent("rows", link_rows, partner)


def deliver(*refs):
    sems = refs[-1]
    moves = [pltpu.make_async_copy(refs[at], refs[4 + at], sems.at[at]) for at in range(4)]
    for move in moves:
        move.start()
    for move in moves:
        move.wait()


def body(*arrays):
    *arrays, ancestors = arrays
    vmem = pl.BlockSpec(memory_space=pltpu.VMEM)
    hbm = pl.BlockSpec(memory_space=pltpu.HBM)
    shape = jax.ShapeDtypeStruct
    sizes = ((B, B), (B, B), (H, B), (B, B))
    held = pl.pallas_call(
        kernel,
        out_shape=tuple(pltpu.VMEM(size, F32) for size in sizes),
        in_specs=[hbm] * 6,
        out_specs=(vmem,) * 4,
        scratch_shapes=[
            pltpu.SMEM((2, 32), jnp.int32),
            pltpu.VMEM((B, 4 * B), F32),
            pltpu.VMEM((4 * B, B), F32),
            pltpu.VMEM((B, B), F32),
            pltpu.VMEM((B, B), F32),
            pltpu.VMEM((B, B), F32),
            pltpu.SemaphoreType.DMA((12,)),
            pltpu.VMEM((B, 4 * B), BF16),
            pltpu.VMEM((B, 4 * B), BF16),
            pltpu.VMEM((CH, 4 * B, 2 * W), BF16),
            pltpu.VMEM((B, 2 * B), BF16),
            pltpu.VMEM((B, B), BF16),
            pltpu.VMEM((B, B), BF16),
            pltpu.VMEM((CH, 4, 2, H, W), F32),
            pltpu.VMEM((CH, 3, 2, H, W), F32),
            pltpu.VMEM((CH, 2, H, W), F32),
            pltpu.VMEM((CH, 2, H, W), F32),
            pltpu.VMEM((CH, 4, 2, H, W), F32),
            pltpu.VMEM((4, 4, 2, H, B), F32),
            pltpu.VMEM((4, 4, H, B), F32),
            pltpu.VMEM((2, 2, H, B), F32),
            pltpu.VMEM((2, 2, H, B), F32),
            pltpu.VMEM((2, 2, H, B), F32),
            pltpu.VMEM((4, H, B), F32),
            pltpu.VMEM((3, H, B), F32),
            pltpu.VMEM((CH, H, W), F32),
            pltpu.VMEM((8, H, B), F32),
            pltpu.VMEM((H, B), F32),
            pltpu.VMEM((W, B), F32),
            pltpu.VMEM((CH, 2, 3, S, W), F32),
            pltpu.VMEM((CH, 3, S, W), F32),
            pltpu.VMEM((CH, 3, S, W), F32),
            pltpu.VMEM((CH, 3, S, W), F32),
            pltpu.VMEM((CH, 8, S, W), F32),
            pltpu.VMEM((CH, 2, 4, 2, 4, S, W), F32),
            pltpu.SemaphoreType.DMA((SENDS,)),
            pltpu.SemaphoreType.DMA((RECVS,)),
        ],
        compiler_params=pltpu.CompilerParams(
            collective_id=0, has_side_effects=True, vmem_limit_bytes=44 * 1024 * 1024
        ),
    )(*[pltpu.with_memory_space_constraint(given, pltpu.HBM) for given in (ancestors, *arrays)])
    held = [pltpu.with_memory_space_constraint(made, pltpu.VMEM) for made in held]
    return pl.pallas_call(
        deliver,
        out_shape=tuple(shape(size, F32) for size in sizes),
        in_specs=[vmem] * 4,
        out_specs=(hbm,) * 4,
        scratch_shapes=[pltpu.SemaphoreType.DMA((4,))],
    )(*held)


def solution(mesh):
    placed = (P("pcol", "prow"), P("prow", None), P("pcol", None), P(), P(), P())
    return jax.shard_map(
        body,
        mesh=mesh,
        in_specs=placed,
        out_specs=(P("pcol", None), P(), P(("prow", "pcol"), None), P()),
        check_vma=False,
    )
```

```python
import functools

import jax
import jax.numpy as jnp
from jax import lax
from jax.experimental import pallas as pl
from jax.experimental.pallas import tpu as pltpu
from jax.sharding import PartitionSpec as P

MESH = pl.DeviceIdType.MESH
F32 = jnp.float32
BF16 = jnp.bfloat16
B = 384
CH = 3
W = 128
H = 48
S = 16
SENDS = 13
RECVS = 46
ROWS = (((0,), (0,)), ((), ()))
PLAIN = (((1,), (0,)), ((), ()))


def split(value):
    high = value.astype(BF16)
    low = (value - high.astype(F32)).astype(BF16)
    return high, low


def mul(left, right, dims=PLAIN):
    return lax.dot_general(left, right, dims, preferred_element_type=F32)


def product(left, right, dims=PLAIN):
    left_high, left_low = left
    right_high, right_low = right
    return mul(left_high, right_high, dims) + (mul(left_high, right_low, dims) + mul(left_low, right_high, dims))


class Copies:
    def __init__(self, send_sems, recv_sems):
        self.send_sems, self.recv_sems = send_sems, recv_sems
        self.kinds, self.keys = {}, {}

    def recv_sem(self, key):
        return self.recv_sems.at[self.keys.setdefault(key, len(self.keys))]

    def make(self, key, src, dst, device):
        return pltpu.make_async_remote_copy(
            src_ref=src,
            dst_ref=dst,
            send_sem=self.send_sems.at[self.kinds.setdefault(key[0], len(self.kinds))],
            recv_sem=self.recv_sem(key),
            device_id=device,
            device_id_type=MESH,
        )

    def send(self, key, src, dst, device):
        self.make(key, src, dst, device).start()

    def wait(self, key, every, device):
        self.make(key, every, every, device).wait_recv()

    def sent(self, kind, every):
        sem = self.send_sems.at[self.kinds[kind]]
        pltpu.make_async_copy(every, every, sem).wait()


class Ring:
    def __init__(self, copies, name, pos, plus, minus, get):
        self.copies, self.name, self.pos, self.plus, self.minus, self.get = copies, name, pos, plus, minus, get

    def at(self, offset, half):
        return self.get(lax.rem(self.pos + offset, 4), half)


class Scatter(Ring):
    def __init__(self, copies, name, pos, plus, minus, get, relay, direct, final):
        super().__init__(copies, name, pos, plus, minus, get)
        self.relayed, self.direct, self.final = relay, direct, final

    def start(self):
        self.start_far()
        self.start_plus()
        self.start_minus()

    def start_far(self):
        self.copies.send((self.name, 0), self.at(2, 0), self.relayed(0), self.plus)
        self.copies.send((self.name, 1), self.at(2, 1), self.relayed(1), self.minus)

    def start_plus(self):
        self.copies.send((self.name, 2), self.at(1, 1), self.direct(0), self.plus)

    def start_minus(self):
        self.copies.send((self.name, 3), self.at(3, 0), self.direct(1), self.minus)

    def relay(self):
        self.copies.wait((self.name, 0), self.relayed(0), self.minus)
        mine = self.at(1, 0)
        mine[...] = mine[...] + self.relayed(0)[...]
        self.copies.send((self.name, 4), mine, self.final(0), self.plus)
        self.copies.wait((self.name, 1), self.relayed(1), self.plus)
        mine = self.at(3, 1)
        mine[...] = mine[...] + self.relayed(1)[...]
        self.copies.send((self.name, 5), mine, self.final(1), self.minus)

    def finish(self):
        self.copies.wait((self.name, 2), self.direct(0), self.minus)
        self.copies.wait((self.name, 3), self.direct(1), self.plus)
        self.copies.wait((self.name, 4), self.final(0), self.minus)
        self.copies.wait((self.name, 5), self.final(1), self.plus)
        first = self.at(0, 0)[...] + (self.direct(1)[...] + self.final(0)[...])
        second = self.at(0, 1)[...] + (self.direct(0)[...] + self.final(1)[...])
        return first, second


class Exchange:
    def __init__(self, copies, key, pos, size, device, src, dst, every):
        self.copies, self.key, self.pos, self.size, self.device = copies, key, pos, size, device
        self.src, self.dst, self.every = src, dst, every
        self.steps = [2, 1, 3] if size == 4 else [4, 3, 5, 2, 6, 1, 7]

    def start(self):
        for step in self.steps:
            there = lax.rem(self.pos + step, self.size)
            self.copies.send(self.key, self.src(there), self.dst(step), self.device(there))

    def finish(self):
        self.copies.wait(self.key, self.every, self.device(lax.rem(self.pos + 1, self.size)))


def kernel(
    marks_hbm, inv_hbm, pan1_hbm, pan2_hbm, link_hbm, diag_hbm, column_first, diag_first, column_second, corner,
    marks, inv, pan1, pan2, link, diag, load_sems, inv_high, inv_low, pan1_cat, pan2_cat, link_high, link_low,
    part, part_in, quarter, quarter_in, column,
    wide, wide_in, wide_relay, wide_direct, wide_final, mine, mine_in, link_rows,
    turned, turned_in, cross, pair, slices_in, depth, grid,
    send_sems, recv_sems,
):
    row, col = lax.axis_index("prow"), lax.axis_index("pcol")
    y, zh = lax.rem(row, 4), lax.div(row, 4)
    x, zl, core = lax.div(col, 8), lax.rem(lax.div(col, 2), 4), lax.rem(col, 2)
    z = zh * 4 + zl

    def device(y=y, zh=zh, x=x, zl=zl, core=core):
        return (zh * 4 + y, (x * 4 + zl) * 2 + core)

    def turn(value, step, size=4):
        return lax.rem(value + step, size)

    def at_z(there):
        return device(zh=lax.div(there, 4), zl=lax.rem(there, 4))

    def at_y(there):
        return device(y=there)

    def at_x(there):
        return device(x=there)

    y_plus, y_minus = device(y=turn(y, 1)), device(y=turn(y, 3))
    x_plus, x_minus = device(x=turn(x, 1)), device(x=turn(x, 3))

    loads = []
    for block in range(4):
        at = pl.ds(block * B, B)
        loads.append((pan1_hbm.at[at, :], pan1.at[at, :]))
        loads.append((inv_hbm.at[:, at], inv.at[:, at]))
    loads += [(pan2_hbm, pan2), (link_hbm, link), (diag_hbm, diag), (marks_hbm, marks)]
    loads = [pltpu.make_async_copy(src, dst, load_sems.at[at]) for at, (src, dst) in enumerate(loads)]

    partner = device(core=1 - core)
    opposite = at_z(turn(z, 4, 8))
    def unless_me(there):
        return jnp.logical_not(jnp.logical_and(there[0] == row, there[1] == col))

    rows_to = (lax.div(col, 4), lax.rem(col, 4) * 8 + y * 2 + zh)
    rows_from = (lax.rem(col, 2) * 4 + lax.div(lax.rem(col, 8), 2), row * 4 + lax.div(col, 8))
    slice_to = (lax.rem(col, 8), row * 4 + lax.div(col, 8))
    slice_from = (lax.div(col, 4), lax.rem(col, 4) * 8 + row)
    rows_move, slice_move = unless_me(rows_to), unless_me(slice_to)

    barrier = pltpu.get_barrier_semaphore()

    def greet(there):
        pl.semaphore_signal(barrier, inc=1, device_id=there, device_id_type=MESH)

    loads[11].start()
    for step in (1, 2, 3):
        greet(at_y(turn(y, step)))
        greet(at_x(turn(x, step)))
        greet(device(x=turn(x, step), core=1 - core))
    greet(partner)
    for step in range(1, 8):
        greet(at_z(turn(z, step, 8)))

    @pl.when(rows_move)
    def _():
        greet(rows_from)

    @pl.when(slice_move)
    def _():
        greet(slice_from)

    for load in loads[0:8:2] + loads[1:8:2]:
        load.start()

    copies = Copies(send_sems, recv_sems)

    def permute(key, src, dst, there, moved):
        remote = copies.make(key, src, dst, there)
        local = pltpu.make_async_copy(src, dst, copies.recv_sem(key))

        @pl.when(moved)
        def _():
            remote.start()

        @pl.when(jnp.logical_not(moved))
        def _():
            local.start()

    for load in loads[0:8:2]:
        load.wait()

    block = pan1[pl.ds(pl.multiple_of(lax.div(col, 8) * B, B), B), :]
    turned[...] = block.T.reshape(8, H, B)
    loads[11].wait()
    first_own = marks[0, col].astype(F32)
    second_own = marks[1, col].astype(F32)
    early = []
    for block in range(4):
        at = slice(block * B, (block + 1) * B)
        scaled = pan1[at, :] * marks[0, row * 4 + block].astype(F32)
        high, low = split(scaled)
        for chunk in range(CH):
            lanes = slice(chunk * W, (chunk + 1) * W)
            pan1_cat[chunk, at, 0:W] = high[:, lanes]
            pan1_cat[chunk, at, W : 2 * W] = low[:, lanes]
        loads[2 * block + 1].wait()
        inv_high[:, at], inv_low[:, at] = split(inv[:, at])
        both = mul(inv_high[:, at], pan1_cat[0, at, :])
        rest = mul(inv_low[:, at], pan1_cat[0, at, 0:W])
        early.append(both[:, 0:W] + (both[:, W : 2 * W] + rest))
    total = ((early[0] + early[1]) + (early[2] + early[3])) * (-first_own)
    part[0] = total.reshape(4, 2, H, W)
    for load in loads[8:11]:
        load.start()

    def partial_product(chunk):
        both = mul(inv_high[...], pan1_cat[chunk])
        rest = mul(inv_low[...], pan1_cat[chunk, :, 0:W])
        total = (both[:, 0:W] + (both[:, W : 2 * W] + rest)) * (-first_own)
        part[chunk] = total.reshape(4, 2, H, W)

    scatter, gather, along_x, along_z, gather_x, gather_y = [], [], [], [], [], []
    for chunk in range(CH):
        for half in range(2):
            scatter.append(
                Exchange(
                    copies, ("part", chunk, half), y, 4, at_y,
                    lambda there, k=chunk, h=half: part.at[k, there, h],
                    lambda step, k=chunk, h=half: part_in.at[k, h, step - 1],
                    part_in.at[chunk, half],
                )
            )
            gather.append(
                Exchange(
                    copies, ("column", chunk, half), y, 4, at_y,
                    lambda there, k=chunk, h=half: column.at[k, y, h],
                    lambda step, k=chunk, h=half: column.at[k, y, h],
                    column.at[chunk, pl.ds(0, 3), half],
                )
            )
        along_x.append(
            Exchange(
                copies, ("slices", chunk), x * 2 + core, 8,
                lambda there: device(x=lax.div(there, 2), core=lax.rem(there, 2)),
                lambda there, k=chunk: pair.at[k, lax.rem(there, 2), jnp.minimum(lax.div(there, 2), 2)],
                lambda step, k=chunk: slices_in.at[k, step - 1],
                slices_in.at[chunk],
            )
        )
        along_z.append(
            Exchange(
                copies, ("depth", chunk), z, 8, at_z,
                lambda there, k=chunk: depth.at[k, z],
                lambda step, k=chunk: depth.at[k, z],
                depth.at[chunk, pl.ds(0, 7)],
            )
        )
        gather_x.append(
            Exchange(
                copies, ("grid_x", chunk), x, 4, at_x,
                lambda there, k=chunk: grid.at[k, core, y, :, x],
                lambda step, k=chunk: grid.at[k, core, y, :, x],
                grid.at[chunk, core, pl.ds(0, 3), :, 0],
            )
        )
        gather_y.append(
            Exchange(
                copies, ("grid_y", chunk), y, 4, at_y,
                lambda there, k=chunk: grid.at[k, core, y, :, pl.ds(0, 3)],
                lambda step, k=chunk: grid.at[k, core, y, :, pl.ds(0, 3)],
                grid.at[chunk, core, pl.ds(0, 3), :, pl.ds(0, 3)],
            )
        )
    across = Scatter(
        copies, "wide", x, x_plus, x_minus,
        lambda q, h: wide.at[q, pl.ds(2 * h, 2), core],
        lambda h: wide_relay.at[h],
        lambda h: wide_direct.at[h],
        lambda h: wide_final.at[h],
    )
    line = Exchange(
        copies, ("line", 0), zl, 4, lambda there: device(zl=there),
        lambda there: mine.at[there],
        lambda step: mine_in.at[step - 1],
        mine_in,
    )

    pl.semaphore_wait(barrier, 17 + jnp.where(rows_move, 1, 0) + jnp.where(slice_move, 1, 0))
    scatter[0].start()
    scatter[1].start()

    partial_product(1)
    scatter[2].start()
    scatter[3].start()
    partial_product(2)
    scatter[4].start()
    scatter[5].start()
    permute(("turned", 0), turned.at[lax.rem(col, 8)], turned_in, slice_to, slice_move)
    loads[8].wait()
    high, low = split(pan2[...] * second_own)
    pan2_cat[:, 0:B] = high
    pan2_cat[:, B : 2 * B] = low

    def wide_product(step):
        there = turn(x, step)
        at = pl.ds(pl.multiple_of(there * B, B), B)
        both = mul(inv_high[:, at], pan2_cat[...], ROWS)
        rest = mul(inv_low[:, at], pan2_cat[:, 0:B], ROWS)
        total = both[:, 0:B] + (both[:, B : 2 * B] + rest)
        wide[there] = total.reshape(4, 2, H, B)
        copies.send(("pairs", step), wide.at[there, :, 1 - core], wide_in.at[there], partner)

    def wide_ready(step):
        there = turn(x, step)
        copies.wait(("pairs", step), wide_in.at[there], partner)
        for lo in range(4):
            wide[there, lo, core] = wide[there, lo, core] + wide_in[there, lo]

    def to_opposite(chunk, half):
        scatter[2 * chunk + half].finish()
        quarter[chunk, half] = (part[chunk, y, half] + part_in[chunk, half, 0]) + (
            part_in[chunk, half, 1] + part_in[chunk, half, 2]
        )
        copies.send(("half", chunk, half), quarter.at[chunk, half], quarter_in.at[chunk, half], opposite)

    wide_product(2)
    to_opposite(0, 0)
    to_opposite(0, 1)
    wide_product(1)
    wide_ready(2)
    across.start_far()
    to_opposite(1, 0)
    to_opposite(1, 1)
    wide_product(3)
    wide_ready(1)
    across.start_plus()
    to_opposite(2, 0)
    to_opposite(2, 1)
    wide_product(0)
    wide_ready(3)
    across.start_minus()
    loads[9].wait()
    loads[10].wait()
    link_high[...], link_low[...] = split(link[...])
    for chunk in range(CH):
        for half in range(2):
            copies.wait(("half", chunk, half), quarter_in.at[chunk, half], opposite)
            column[chunk, y, half] = quarter[chunk, half] + quarter_in[chunk, half]
            gather[2 * chunk + half].start()

    copies.wait(("turned", 0), turned_in, partner)
    turned_high, turned_low = split(turned_in[...])

    for chunk in range(CH):
        gather[2 * chunk].finish()
        gather[2 * chunk + 1].finish()
        whole = column[chunk].reshape(B, W)
        column_first[:, chunk * W : (chunk + 1) * W] = whole
        whole = split(whole)
        slice_first = product((turned_high, turned_low), whole)
        both = mul(whole[0], pan2_cat[...], ROWS)
        rest = mul(whole[1], pan2_cat[:, 0:B], ROWS)
        cross[...] = both[:, 0:B] + (both[:, B : 2 * B] + rest)
        pair[chunk, 0] = slice_first.reshape(3, S, W)
        for third in range(3):
            pair[chunk, 1, third] = cross[pl.ds(pl.multiple_of(row * S, S), S), third * W : (third + 1) * W]
        along_x[chunk].start()
        if chunk == 0:
            wide_ready(0)
            across.relay()
    for chunk in range(CH):
        along_x[chunk].finish()
        total = pair[chunk, core, jnp.minimum(x, 2)] + slices_in[chunk, 0]
        for step in range(1, 7):
            total = total + slices_in[chunk, step]
        depth[chunk, z] = total
        along_z[chunk].start()

    permute(("rows", 0), column.at[:, y, zh], link_rows, rows_to, rows_move)
    for chunk in range(CH):
        along_z[chunk].finish()
        for half in range(2):
            grid[chunk, core, y, half, x] = (
                (depth[chunk, 4 * half] + depth[chunk, 4 * half + 1]) + depth[chunk, 4 * half + 2]
            ) + depth[chunk, 4 * half + 3]
        gather_x[chunk].start()

    mine[0:2], mine[2:4] = across.finish()
    line.start()

    def pass_on(chunk, step):
        part_at = grid.at[chunk, core, turn(y, step), :, pl.ds(0, 3)]
        copies.send(("swap", chunk), part_at, part_at, partner)

    for chunk in range(CH):
        gather_x[chunk].finish()
        gather_y[chunk].start()
        pass_on(chunk, 0)
    for chunk in range(CH):
        gather_y[chunk].finish()
        for step in (1, 3, 2):
            pass_on(chunk, step)

    line.finish()
    copies.wait(("rows", 0), link_rows, partner)
    block_row = row * 4 + lax.div(col, 8)
    rows_here = jnp.concatenate([link_rows[chunk] for chunk in range(CH)], axis=1)
    total = (mine[zl] + mine_in[0]) + (mine_in[1] + mine_in[2])
    total = total + product(split(rows_here), (link_high[...], link_low[...]))
    column_second[...] = total * (-marks[1, block_row].astype(F32))

    linked = []
    for chunk in range(CH):
        copies.wait(("swap", chunk), grid.at[chunk, 1 - core, :, :, pl.ds(0, 3)], partner)
        lanes = slice(chunk * W, (chunk + 1) * W)
        for piece in range(8):
            at = slice(piece * H, (piece + 1) * H)
            found = grid[chunk, 0, piece % 4, piece // 4, 0:3].reshape(H, W)
            diag_first[at, lanes] = diag[at, lanes] - found
        ready = split(diag_first[:, lanes])
        linked.append(product(ready, (link_high[lanes, :], link_low[lanes, :])))
    total = linked[0] + (linked[1] + linked[2])
    for chunk in range(CH):
        for piece in range(8):
            at = slice(chunk * W + piece * S, chunk * W + (piece + 1) * S)
            for third in range(3):
                lanes = slice(third * W, (third + 1) * W)
                corner[at, lanes] = -(total[at, lanes] + grid[chunk, 1, piece % 4, piece // 4, third])

    for kind, every in (
        ("part", part.at[:, pl.ds(0, 3)]),
        ("half", quarter),
        ("column", column.at[:, pl.ds(0, 3)]),
        ("pairs", wide_in),
        ("wide", wide.at[pl.ds(0, 3), :, 0]),
        ("line", mine_in),
        ("slices", slices_in),
        ("depth", depth.at[:, pl.ds(0, 7)]),
        ("grid_x", grid.at[:, 0, pl.ds(0, 3), :, 0]),
        ("grid_y", grid.at[:, 0, pl.ds(0, 3), :, pl.ds(0, 3)]),
        ("swap", grid.at[:, 0, :, :, pl.ds(0, 3)]),
    ):
        copies.sent(kind, every)

    @pl.when(slice_move)
    def _():
        copies.sent("turned", turned_in)

    @pl.when(rows_move)
    def _():
        copies.sent("rows", link_rows)


def deliver(*refs):
    sems = refs[-1]
    moves = [pltpu.make_async_copy(refs[at], refs[4 + at], sems.at[at]) for at in range(4)]
    for move in moves:
        move.start()
    for move in moves:
        move.wait()


def body(*arrays):
    *arrays, ancestors = arrays
    vmem = pl.BlockSpec(memory_space=pltpu.VMEM)
    hbm = pl.BlockSpec(memory_space=pltpu.HBM)
    shape = jax.ShapeDtypeStruct
    sizes = ((B, B), (B, B), (H, B), (B, B))
    held = pl.pallas_call(
        kernel,
        out_shape=tuple(pltpu.VMEM(size, F32) for size in sizes),
        in_specs=[hbm] * 6,
        out_specs=(vmem,) * 4,
        scratch_shapes=[
            pltpu.SMEM((2, 32), jnp.int32),
            pltpu.VMEM((B, 4 * B), F32),
            pltpu.VMEM((4 * B, B), F32),
            pltpu.VMEM((B, B), F32),
            pltpu.VMEM((B, B), F32),
            pltpu.VMEM((B, B), F32),
            pltpu.SemaphoreType.DMA((12,)),
            pltpu.VMEM((B, 4 * B), BF16),
            pltpu.VMEM((B, 4 * B), BF16),
            pltpu.VMEM((CH, 4 * B, 2 * W), BF16),
            pltpu.VMEM((B, 2 * B), BF16),
            pltpu.VMEM((B, B), BF16),
            pltpu.VMEM((B, B), BF16),
            pltpu.VMEM((CH, 4, 2, H, W), F32),
            pltpu.VMEM((CH, 2, 3, H, W), F32),
            pltpu.VMEM((CH, 2, H, W), F32),
            pltpu.VMEM((CH, 2, H, W), F32),
            pltpu.VMEM((CH, 4, 2, H, W), F32),
            pltpu.VMEM((4, 4, 2, H, B), F32),
            pltpu.VMEM((4, 4, H, B), F32),
            pltpu.VMEM((2, 2, H, B), F32),
            pltpu.VMEM((2, 2, H, B), F32),
            pltpu.VMEM((2, 2, H, B), F32),
            pltpu.VMEM((4, H, B), F32),
            pltpu.VMEM((3, H, B), F32),
            pltpu.VMEM((CH, H, W), F32),
            pltpu.VMEM((8, H, B), F32),
            pltpu.VMEM((H, B), F32),
            pltpu.VMEM((W, B), F32),
            pltpu.VMEM((CH, 2, 3, S, W), F32),
            pltpu.VMEM((CH, 7, S, W), F32),
            pltpu.VMEM((CH, 8, S, W), F32),
            pltpu.VMEM((CH, 2, 4, 2, 4, S, W), F32),
            pltpu.SemaphoreType.DMA((SENDS,)),
            pltpu.SemaphoreType.DMA((RECVS,)),
        ],
        compiler_params=pltpu.CompilerParams(
            collective_id=0, has_side_effects=True, vmem_limit_bytes=44 * 1024 * 1024
        ),
    )(*[pltpu.with_memory_space_constraint(given, pltpu.HBM) for given in (ancestors, *arrays)])
    held = [pltpu.with_memory_space_constraint(made, pltpu.VMEM) for made in held]
    return pl.pallas_call(
        deliver,
        out_shape=tuple(shape(size, F32) for size in sizes),
        in_specs=[vmem] * 4,
        out_specs=(hbm,) * 4,
        scratch_shapes=[pltpu.SemaphoreType.DMA((4,))],
    )(*held)


def solution(mesh):
    placed = (P("pcol", "prow"), P("prow", None), P("pcol", None), P(), P(), P())
    return jax.shard_map(
        body,
        mesh=mesh,
        in_specs=placed,
        out_specs=(P("pcol", None), P(), P(("prow", "pcol"), None), P()),
        check_vma=False,
    )
```

```python
import functools

import jax
import jax.numpy as jnp
from jax import lax
from jax.experimental import pallas as pl
from jax.experimental.pallas import tpu as pltpu
from jax.sharding import PartitionSpec as P

MESH = pl.DeviceIdType.MESH
F32 = jnp.float32
BF16 = jnp.bfloat16
B = 384
CH = 3
W = 128
H = 48
S = 16
SENDS = 13
RECVS = 46
ROWS = (((0,), (0,)), ((), ()))
PLAIN = (((1,), (0,)), ((), ()))


def split(value):
    high = value.astype(BF16)
    low = (value - high.astype(F32)).astype(BF16)
    return high, low


def mul(left, right, dims=PLAIN):
    return lax.dot_general(left, right, dims, preferred_element_type=F32)


def product(left, right, dims=PLAIN):
    left_high, left_low = left
    right_high, right_low = right
    return mul(left_high, right_high, dims) + (mul(left_high, right_low, dims) + mul(left_low, right_high, dims))


class Copies:
    def __init__(self, send_sems, recv_sems):
        self.send_sems, self.recv_sems = send_sems, recv_sems
        self.kinds, self.keys = {}, {}

    def recv_sem(self, key):
        return self.recv_sems.at[self.keys.setdefault(key, len(self.keys))]

    def make(self, key, src, dst, device):
        return pltpu.make_async_remote_copy(
            src_ref=src,
            dst_ref=dst,
            send_sem=self.send_sems.at[self.kinds.setdefault(key[0], len(self.kinds))],
            recv_sem=self.recv_sem(key),
            device_id=device,
            device_id_type=MESH,
        )

    def send(self, key, src, dst, device):
        self.make(key, src, dst, device).start()

    def wait(self, key, every, device):
        self.make(key, every, every, device).wait_recv()

    def sent(self, kind, every):
        sem = self.send_sems.at[self.kinds[kind]]
        pltpu.make_async_copy(every, every, sem).wait()


class Ring:
    def __init__(self, copies, name, pos, plus, minus, get):
        self.copies, self.name, self.pos, self.plus, self.minus, self.get = copies, name, pos, plus, minus, get

    def at(self, offset, half):
        return self.get(lax.rem(self.pos + offset, 4), half)


class Scatter(Ring):
    def __init__(self, copies, name, pos, plus, minus, get, relay, direct, final):
        super().__init__(copies, name, pos, plus, minus, get)
        self.relayed, self.direct, self.final = relay, direct, final

    def start(self):
        self.start_far()
        self.start_plus()
        self.start_minus()

    def start_far(self):
        self.copies.send((self.name, 0), self.at(2, 0), self.relayed(0), self.plus)
        self.copies.send((self.name, 1), self.at(2, 1), self.relayed(1), self.minus)

    def start_plus(self):
        self.copies.send((self.name, 2), self.at(1, 1), self.direct(0), self.plus)

    def start_minus(self):
        self.copies.send((self.name, 3), self.at(3, 0), self.direct(1), self.minus)

    def relay(self):
        self.copies.wait((self.name, 0), self.relayed(0), self.minus)
        mine = self.at(1, 0)
        mine[...] = mine[...] + self.relayed(0)[...]
        self.copies.send((self.name, 4), mine, self.final(0), self.plus)
        self.copies.wait((self.name, 1), self.relayed(1), self.plus)
        mine = self.at(3, 1)
        mine[...] = mine[...] + self.relayed(1)[...]
        self.copies.send((self.name, 5), mine, self.final(1), self.minus)

    def finish(self):
        self.copies.wait((self.name, 2), self.direct(0), self.minus)
        self.copies.wait((self.name, 3), self.direct(1), self.plus)
        self.copies.wait((self.name, 4), self.final(0), self.minus)
        self.copies.wait((self.name, 5), self.final(1), self.plus)
        first = self.at(0, 0)[...] + (self.direct(1)[...] + self.final(0)[...])
        second = self.at(0, 1)[...] + (self.direct(0)[...] + self.final(1)[...])
        return first, second


class Exchange:
    def __init__(self, copies, key, pos, size, device, src, dst, every):
        self.copies, self.key, self.pos, self.size, self.device = copies, key, pos, size, device
        self.src, self.dst, self.every = src, dst, every
        self.steps = [2, 1, 3] if size == 4 else [4, 3, 5, 2, 6, 1, 7]

    def start(self):
        for step in self.steps:
            there = lax.rem(self.pos + step, self.size)
            self.copies.send(self.key, self.src(there), self.dst(step), self.device(there))

    def finish(self):
        self.copies.wait(self.key, self.every, self.device(lax.rem(self.pos + 1, self.size)))


def kernel(
    marks_hbm, inv_hbm, pan1_hbm, pan2_hbm, link_hbm, diag_hbm, column_first, diag_first, column_second, corner,
    marks, inv, pan1, pan2, link, diag, load_sems, inv_high, inv_low, pan1_cat, pan2_cat, link_high, link_low,
    part, part_in, quarter, quarter_in, column,
    wide, wide_in, wide_relay, wide_direct, wide_final, mine, mine_in, link_rows,
    turned, turned_in, cross, pair, slices_in, depth, grid,
    send_sems, recv_sems,
):
    row, col = lax.axis_index("prow"), lax.axis_index("pcol")
    y, zh = lax.rem(row, 4), lax.div(row, 4)
    x, zl, core = lax.div(col, 8), lax.rem(lax.div(col, 2), 4), lax.rem(col, 2)
    z = zh * 4 + zl

    def device(y=y, zh=zh, x=x, zl=zl, core=core):
        return (zh * 4 + y, (x * 4 + zl) * 2 + core)

    def turn(value, step, size=4):
        return lax.rem(value + step, size)

    def at_z(there):
        return device(zh=lax.div(there, 4), zl=lax.rem(there, 4))

    def at_y(there):
        return device(y=there)

    def at_x(there):
        return device(x=there)

    y_plus, y_minus = device(y=turn(y, 1)), device(y=turn(y, 3))
    x_plus, x_minus = device(x=turn(x, 1)), device(x=turn(x, 3))

    loads = []
    for block in range(4):
        at = pl.ds(block * B, B)
        loads.append((pan1_hbm.at[at, :], pan1.at[at, :]))
        loads.append((inv_hbm.at[:, at], inv.at[:, at]))
    loads += [(pan2_hbm, pan2), (link_hbm, link), (diag_hbm, diag), (marks_hbm, marks)]
    loads = [pltpu.make_async_copy(src, dst, load_sems.at[at]) for at, (src, dst) in enumerate(loads)]

    partner = device(core=1 - core)
    opposite = at_z(turn(z, 4, 8))
    def unless_me(there):
        return jnp.logical_not(jnp.logical_and(there[0] == row, there[1] == col))

    rows_to = (lax.div(col, 4), lax.rem(col, 4) * 8 + y * 2 + zh)
    rows_from = (lax.rem(col, 2) * 4 + lax.div(lax.rem(col, 8), 2), row * 4 + lax.div(col, 8))
    slice_to = (lax.rem(col, 8), row * 4 + lax.div(col, 8))
    slice_from = (lax.div(col, 4), lax.rem(col, 4) * 8 + row)
    rows_move, slice_move = unless_me(rows_to), unless_me(slice_to)

    barrier = pltpu.get_barrier_semaphore()

    def greet(there):
        pl.semaphore_signal(barrier, inc=1, device_id=there, device_id_type=MESH)

    loads[11].start()
    for step in (1, 2, 3):
        greet(at_y(turn(y, step)))
        greet(at_x(turn(x, step)))
        greet(device(x=turn(x, step), core=1 - core))
    greet(partner)
    for step in range(1, 8):
        greet(at_z(turn(z, step, 8)))

    @pl.when(rows_move)
    def _():
        greet(rows_from)

    @pl.when(slice_move)
    def _():
        greet(slice_from)

    for load in loads[0:8:2] + loads[1:8:2]:
        load.start()

    copies = Copies(send_sems, recv_sems)

    def permute(key, src, dst, there, moved):
        remote = copies.make(key, src, dst, there)
        local = pltpu.make_async_copy(src, dst, copies.recv_sem(key))

        @pl.when(moved)
        def _():
            remote.start()

        @pl.when(jnp.logical_not(moved))
        def _():
            local.start()

    for load in loads[0:8:2]:
        load.wait()

    block = pan1[pl.ds(pl.multiple_of(lax.div(col, 8) * B, B), B), :]
    turned[...] = block.T.reshape(8, H, B)
    loads[11].wait()
    first_own = marks[0, col].astype(F32)
    second_own = marks[1, col].astype(F32)
    early = []
    for block in range(4):
        at = slice(block * B, (block + 1) * B)
        scaled = pan1[at, :] * marks[0, row * 4 + block].astype(F32)
        high, low = split(scaled)
        for chunk in range(CH):
            lanes = slice(chunk * W, (chunk + 1) * W)
            pan1_cat[chunk, at, 0:W] = high[:, lanes]
            pan1_cat[chunk, at, W : 2 * W] = low[:, lanes]
        loads[2 * block + 1].wait()
        inv_high[:, at], inv_low[:, at] = split(inv[:, at])
        both = mul(inv_high[:, at], pan1_cat[0, at, :])
        rest = mul(inv_low[:, at], pan1_cat[0, at, 0:W])
        early.append(both[:, 0:W] + (both[:, W : 2 * W] + rest))
    total = ((early[0] + early[1]) + (early[2] + early[3])) * (-first_own)
    part[0] = total.reshape(4, 2, H, W)
    for load in loads[8:11]:
        load.start()

    def partial_product(chunk):
        both = mul(inv_high[...], pan1_cat[chunk])
        rest = mul(inv_low[...], pan1_cat[chunk, :, 0:W])
        total = (both[:, 0:W] + (both[:, W : 2 * W] + rest)) * (-first_own)
        part[chunk] = total.reshape(4, 2, H, W)

    scatter, gather, along_x, along_z, gather_x, gather_y = [], [], [], [], [], []
    for chunk in range(CH):
        for half in range(2):
            scatter.append(
                Exchange(
                    copies, ("part", chunk, half), y, 4, at_y,
                    lambda there, k=chunk, h=half: part.at[k, there, h],
                    lambda step, k=chunk, h=half: part_in.at[k, h, step - 1],
                    part_in.at[chunk, half],
                )
            )
            gather.append(
                Exchange(
                    copies, ("column", chunk, half), y, 4, at_y,
                    lambda there, k=chunk, h=half: column.at[k, y, h],
                    lambda step, k=chunk, h=half: column.at[k, y, h],
                    column.at[chunk, pl.ds(0, 3), half],
                )
            )
        along_x.append(
            Exchange(
                copies, ("slices", chunk), x * 2 + core, 8,
                lambda there: device(x=lax.div(there, 2), core=lax.rem(there, 2)),
                lambda there, k=chunk: pair.at[k, lax.rem(there, 2), jnp.minimum(lax.div(there, 2), 2)],
                lambda step, k=chunk: slices_in.at[k, step - 1],
                slices_in.at[chunk],
            )
        )
        along_z.append(
            Exchange(
                copies, ("depth", chunk), z, 8, at_z,
                lambda there, k=chunk: depth.at[k, z],
                lambda step, k=chunk: depth.at[k, z],
                depth.at[chunk, pl.ds(0, 7)],
            )
        )
        gather_x.append(
            Exchange(
                copies, ("grid_x", chunk), x, 4, at_x,
                lambda there, k=chunk: grid.at[k, core, y, :, x],
                lambda step, k=chunk: grid.at[k, core, y, :, x],
                grid.at[chunk, core, pl.ds(0, 3), :, 0],
            )
        )
        gather_y.append(
            Exchange(
                copies, ("grid_y", chunk), y, 4, at_y,
                lambda there, k=chunk: grid.at[k, core, y, :, pl.ds(0, 3)],
                lambda step, k=chunk: grid.at[k, core, y, :, pl.ds(0, 3)],
                grid.at[chunk, core, pl.ds(0, 3), :, pl.ds(0, 3)],
            )
        )
    across = Scatter(
        copies, "wide", x, x_plus, x_minus,
        lambda q, h: wide.at[q, pl.ds(2 * h, 2), core],
        lambda h: wide_relay.at[h],
        lambda h: wide_direct.at[h],
        lambda h: wide_final.at[h],
    )
    line = Exchange(
        copies, ("line", 0), zl, 4, lambda there: device(zl=there),
        lambda there: mine.at[there],
        lambda step: mine_in.at[step - 1],
        mine_in,
    )

    pl.semaphore_wait(barrier, 17 + jnp.where(rows_move, 1, 0) + jnp.where(slice_move, 1, 0))
    scatter[0].start()
    scatter[1].start()

    partial_product(1)
    scatter[2].start()
    scatter[3].start()
    partial_product(2)
    scatter[4].start()
    scatter[5].start()
    permute(("turned", 0), turned.at[lax.rem(col, 8)], turned_in, slice_to, slice_move)
    loads[8].wait()
    high, low = split(pan2[...] * second_own)
    pan2_cat[:, 0:B] = high
    pan2_cat[:, B : 2 * B] = low

    def wide_product(step):
        there = turn(x, step)
        at = pl.ds(pl.multiple_of(there * B, B), B)
        both = mul(inv_high[:, at], pan2_cat[...], ROWS)
        rest = mul(inv_low[:, at], pan2_cat[:, 0:B], ROWS)
        total = both[:, 0:B] + (both[:, B : 2 * B] + rest)
        wide[there] = total.reshape(4, 2, H, B)
        copies.send(("pairs", step), wide.at[there, :, 1 - core], wide_in.at[there], partner)

    def wide_ready(step):
        there = turn(x, step)
        copies.wait(("pairs", step), wide_in.at[there], partner)
        for lo in range(4):
            wide[there, lo, core] = wide[there, lo, core] + wide_in[there, lo]

    def to_opposite(chunk, half):
        scatter[2 * chunk + half].finish()
        quarter[chunk, half] = (part[chunk, y, half] + part_in[chunk, half, 0]) + (
            part_in[chunk, half, 1] + part_in[chunk, half, 2]
        )
        copies.send(("half", chunk, half), quarter.at[chunk, half], quarter_in.at[chunk, half], opposite)

    wide_product(2)
    to_opposite(0, 0)
    to_opposite(0, 1)
    wide_product(1)
    wide_ready(2)
    across.start_far()
    to_opposite(1, 0)
    to_opposite(1, 1)
    wide_product(3)
    wide_ready(1)
    across.start_plus()
    to_opposite(2, 0)
    to_opposite(2, 1)
    wide_product(0)
    wide_ready(3)
    across.start_minus()
    loads[9].wait()
    loads[10].wait()
    link_high[...], link_low[...] = split(link[...])
    for chunk in range(CH):
        for half in range(2):
            copies.wait(("half", chunk, half), quarter_in.at[chunk, half], opposite)
            column[chunk, y, half] = quarter[chunk, half] + quarter_in[chunk, half]
            gather[2 * chunk + half].start()

    copies.wait(("turned", 0), turned_in, partner)
    turned_high, turned_low = split(turned_in[...])

    for chunk in range(CH):
        gather[2 * chunk].finish()
        gather[2 * chunk + 1].finish()
        whole = column[chunk].reshape(B, W)
        column_first[:, chunk * W : (chunk + 1) * W] = whole
        whole = split(whole)
        slice_first = product((turned_high, turned_low), whole)
        both = mul(whole[0], pan2_cat[...], ROWS)
        rest = mul(whole[1], pan2_cat[:, 0:B], ROWS)
        cross[...] = both[:, 0:B] + (both[:, B : 2 * B] + rest)
        pair[chunk, 0] = slice_first.reshape(3, S, W)
        for third in range(3):
            pair[chunk, 1, third] = cross[pl.ds(pl.multiple_of(row * S, S), S), third * W : (third + 1) * W]
        along_x[chunk].start()
        if chunk == 0:
            wide_ready(0)
            across.relay()
    for chunk in range(CH):
        along_x[chunk].finish()
        total = pair[chunk, core, jnp.minimum(x, 2)] + slices_in[chunk, 0]
        for step in range(1, 7):
            total = total + slices_in[chunk, step]
        depth[chunk, z] = total
        along_z[chunk].start()

    permute(("rows", 0), column.at[:, y, zh], link_rows, rows_to, rows_move)
    for chunk in range(CH):
        along_z[chunk].finish()
        for half in range(2):
            grid[chunk, core, y, half, x] = (
                (depth[chunk, 4 * half] + depth[chunk, 4 * half + 1]) + depth[chunk, 4 * half + 2]
            ) + depth[chunk, 4 * half + 3]
        gather_x[chunk].start()

    def pass_on(chunk, step):
        part_at = grid.at[chunk, core, turn(y, step), :, pl.ds(0, 3)]
        copies.send(("swap", chunk), part_at, part_at, partner)

    for chunk in range(CH):
        gather_x[chunk].finish()
        gather_y[chunk].start()
        pass_on(chunk, 0)
    mine[0:2], mine[2:4] = across.finish()
    line.start()

    for chunk in range(CH):
        gather_y[chunk].finish()
        for step in (1, 3, 2):
            pass_on(chunk, step)

    line.finish()
    copies.wait(("rows", 0), link_rows, partner)
    block_row = row * 4 + lax.div(col, 8)
    rows_here = jnp.concatenate([link_rows[chunk] for chunk in range(CH)], axis=1)
    total = (mine[zl] + mine_in[0]) + (mine_in[1] + mine_in[2])
    total = total + product(split(rows_here), (link_high[...], link_low[...]))
    column_second[...] = total * (-marks[1, block_row].astype(F32))

    linked = []
    for chunk in range(CH):
        copies.wait(("swap", chunk), grid.at[chunk, 1 - core, :, :, pl.ds(0, 3)], partner)
        lanes = slice(chunk * W, (chunk + 1) * W)
        for piece in range(8):
            at = slice(piece * H, (piece + 1) * H)
            found = grid[chunk, 0, piece % 4, piece // 4, 0:3].reshape(H, W)
            diag_first[at, lanes] = diag[at, lanes] - found
        ready = split(diag_first[:, lanes])
        linked.append(product(ready, (link_high[lanes, :], link_low[lanes, :])))
    total = linked[0] + (linked[1] + linked[2])
    for chunk in range(CH):
        for piece in range(8):
            at = slice(chunk * W + piece * S, chunk * W + (piece + 1) * S)
            for third in range(3):
                lanes = slice(third * W, (third + 1) * W)
                corner[at, lanes] = -(total[at, lanes] + grid[chunk, 1, piece % 4, piece // 4, third])

    for kind, every in (
        ("part", part.at[:, pl.ds(0, 3)]),
        ("half", quarter),
        ("column", column.at[:, pl.ds(0, 3)]),
        ("pairs", wide_in),
        ("wide", wide.at[pl.ds(0, 3), :, 0]),
        ("line", mine_in),
        ("slices", slices_in),
        ("depth", depth.at[:, pl.ds(0, 7)]),
        ("grid_x", grid.at[:, 0, pl.ds(0, 3), :, 0]),
        ("grid_y", grid.at[:, 0, pl.ds(0, 3), :, pl.ds(0, 3)]),
        ("swap", grid.at[:, 0, :, :, pl.ds(0, 3)]),
    ):
        copies.sent(kind, every)

    @pl.when(slice_move)
    def _():
        copies.sent("turned", turned_in)

    @pl.when(rows_move)
    def _():
        copies.sent("rows", link_rows)


def deliver(*refs):
    sems = refs[-1]
    moves = [pltpu.make_async_copy(refs[at], refs[4 + at], sems.at[at]) for at in range(4)]
    for move in moves:
        move.start()
    for move in moves:
        move.wait()


def body(*arrays):
    *arrays, ancestors = arrays
    vmem = pl.BlockSpec(memory_space=pltpu.VMEM)
    hbm = pl.BlockSpec(memory_space=pltpu.HBM)
    shape = jax.ShapeDtypeStruct
    sizes = ((B, B), (B, B), (H, B), (B, B))
    held = pl.pallas_call(
        kernel,
        out_shape=tuple(pltpu.VMEM(size, F32) for size in sizes),
        in_specs=[hbm] * 6,
        out_specs=(vmem,) * 4,
        scratch_shapes=[
            pltpu.SMEM((2, 32), jnp.int32),
            pltpu.VMEM((B, 4 * B), F32),
            pltpu.VMEM((4 * B, B), F32),
            pltpu.VMEM((B, B), F32),
            pltpu.VMEM((B, B), F32),
            pltpu.VMEM((B, B), F32),
            pltpu.SemaphoreType.DMA((12,)),
            pltpu.VMEM((B, 4 * B), BF16),
            pltpu.VMEM((B, 4 * B), BF16),
            pltpu.VMEM((CH, 4 * B, 2 * W), BF16),
            pltpu.VMEM((B, 2 * B), BF16),
            pltpu.VMEM((B, B), BF16),
            pltpu.VMEM((B, B), BF16),
            pltpu.VMEM((CH, 4, 2, H, W), F32),
            pltpu.VMEM((CH, 2, 3, H, W), F32),
            pltpu.VMEM((CH, 2, H, W), F32),
            pltpu.VMEM((CH, 2, H, W), F32),
            pltpu.VMEM((CH, 4, 2, H, W), F32),
            pltpu.VMEM((4, 4, 2, H, B), F32),
            pltpu.VMEM((4, 4, H, B), F32),
            pltpu.VMEM((2, 2, H, B), F32),
            pltpu.VMEM((2, 2, H, B), F32),
            pltpu.VMEM((2, 2, H, B), F32),
            pltpu.VMEM((4, H, B), F32),
            pltpu.VMEM((3, H, B), F32),
            pltpu.VMEM((CH, H, W), F32),
            pltpu.VMEM((8, H, B), F32),
            pltpu.VMEM((H, B), F32),
            pltpu.VMEM((W, B), F32),
            pltpu.VMEM((CH, 2, 3, S, W), F32),
            pltpu.VMEM((CH, 7, S, W), F32),
            pltpu.VMEM((CH, 8, S, W), F32),
            pltpu.VMEM((CH, 2, 4, 2, 4, S, W), F32),
            pltpu.SemaphoreType.DMA((SENDS,)),
            pltpu.SemaphoreType.DMA((RECVS,)),
        ],
        compiler_params=pltpu.CompilerParams(
            collective_id=0, has_side_effects=True, vmem_limit_bytes=44 * 1024 * 1024
        ),
    )(*[pltpu.with_memory_space_constraint(given, pltpu.HBM) for given in (ancestors, *arrays)])
    held = [pltpu.with_memory_space_constraint(made, pltpu.VMEM) for made in held]
    return pl.pallas_call(
        deliver,
        out_shape=tuple(shape(size, F32) for size in sizes),
        in_specs=[vmem] * 4,
        out_specs=(hbm,) * 4,
        scratch_shapes=[pltpu.SemaphoreType.DMA((4,))],
    )(*held)


def solution(mesh):
    placed = (P("pcol", "prow"), P("prow", None), P("pcol", None), P(), P(), P())
    return jax.shard_map(
        body,
        mesh=mesh,
        in_specs=placed,
        out_specs=(P("pcol", None), P(), P(("prow", "pcol"), None), P()),
        check_vma=False,
    )
```

```python
import functools

import jax
import jax.numpy as jnp
from jax import lax
from jax.experimental import pallas as pl
from jax.experimental.pallas import tpu as pltpu
from jax.sharding import PartitionSpec as P

MESH = pl.DeviceIdType.MESH
F32 = jnp.float32
BF16 = jnp.bfloat16
B = 384
CH = 3
W = 128
H = 48
S = 16
SENDS = 13
RECVS = 46
ROWS = (((0,), (0,)), ((), ()))
PLAIN = (((1,), (0,)), ((), ()))


def split(value):
    high = value.astype(BF16)
    low = (value - high.astype(F32)).astype(BF16)
    return high, low


def mul(left, right, dims=PLAIN):
    return lax.dot_general(left, right, dims, preferred_element_type=F32)


def product(left, right, dims=PLAIN):
    left_high, left_low = left
    right_high, right_low = right
    return mul(left_high, right_high, dims) + (mul(left_high, right_low, dims) + mul(left_low, right_high, dims))


class Copies:
    def __init__(self, send_sems, recv_sems):
        self.send_sems, self.recv_sems = send_sems, recv_sems
        self.kinds, self.keys = {}, {}

    def recv_sem(self, key):
        return self.recv_sems.at[self.keys.setdefault(key, len(self.keys))]

    def make(self, key, src, dst, device):
        return pltpu.make_async_remote_copy(
            src_ref=src,
            dst_ref=dst,
            send_sem=self.send_sems.at[self.kinds.setdefault(key[0], len(self.kinds))],
            recv_sem=self.recv_sem(key),
            device_id=device,
            device_id_type=MESH,
        )

    def send(self, key, src, dst, device):
        self.make(key, src, dst, device).start()

    def wait(self, key, every, device):
        self.make(key, every, every, device).wait_recv()

    def sent(self, kind, every):
        sem = self.send_sems.at[self.kinds[kind]]
        pltpu.make_async_copy(every, every, sem).wait()


class Ring:
    def __init__(self, copies, name, pos, plus, minus, get):
        self.copies, self.name, self.pos, self.plus, self.minus, self.get = copies, name, pos, plus, minus, get

    def at(self, offset, half):
        return self.get(lax.rem(self.pos + offset, 4), half)


class Scatter(Ring):
    def __init__(self, copies, name, pos, plus, minus, get, relay, direct, final):
        super().__init__(copies, name, pos, plus, minus, get)
        self.relayed, self.direct, self.final = relay, direct, final

    def start(self):
        self.start_far()
        self.start_plus()
        self.start_minus()

    def start_far(self):
        self.copies.send((self.name, 0), self.at(2, 0), self.relayed(0), self.plus)
        self.copies.send((self.name, 1), self.at(2, 1), self.relayed(1), self.minus)

    def start_plus(self):
        self.copies.send((self.name, 2), self.at(1, 1), self.direct(0), self.plus)

    def start_minus(self):
        self.copies.send((self.name, 3), self.at(3, 0), self.direct(1), self.minus)

    def relay(self):
        self.copies.wait((self.name, 0), self.relayed(0), self.minus)
        mine = self.at(1, 0)
        mine[...] = mine[...] + self.relayed(0)[...]
        self.copies.send((self.name, 4), mine, self.final(0), self.plus)
        self.copies.wait((self.name, 1), self.relayed(1), self.plus)
        mine = self.at(3, 1)
        mine[...] = mine[...] + self.relayed(1)[...]
        self.copies.send((self.name, 5), mine, self.final(1), self.minus)

    def finish(self):
        self.copies.wait((self.name, 2), self.direct(0), self.minus)
        self.copies.wait((self.name, 3), self.direct(1), self.plus)
        self.copies.wait((self.name, 4), self.final(0), self.minus)
        self.copies.wait((self.name, 5), self.final(1), self.plus)
        first = self.at(0, 0)[...] + (self.direct(1)[...] + self.final(0)[...])
        second = self.at(0, 1)[...] + (self.direct(0)[...] + self.final(1)[...])
        return first, second


class Exchange:
    def __init__(self, copies, key, pos, size, device, src, dst, every):
        self.copies, self.key, self.pos, self.size, self.device = copies, key, pos, size, device
        self.src, self.dst, self.every = src, dst, every
        self.steps = [2, 1, 3] if size == 4 else [4, 3, 5, 2, 6, 1, 7]

    def start(self):
        for step in self.steps:
            there = lax.rem(self.pos + step, self.size)
            self.copies.send(self.key, self.src(there), self.dst(step), self.device(there))

    def finish(self):
        self.copies.wait(self.key, self.every, self.device(lax.rem(self.pos + 1, self.size)))


def kernel(
    marks_hbm, inv_hbm, pan1_hbm, pan2_hbm, link_hbm, diag_hbm, column_first, diag_first, column_second, corner,
    marks, inv, pan1, pan2, link, diag, load_sems, inv_high, inv_low, pan1_cat, pan2_cat, link_high, link_low,
    part, part_in, quarter, quarter_in, column,
    wide, wide_in, wide_relay, wide_direct, wide_final, mine, mine_in, link_rows,
    turned, turned_in, cross, pair, slices_in, depth, grid,
    send_sems, recv_sems,
):
    row, col = lax.axis_index("prow"), lax.axis_index("pcol")
    y, zh = lax.rem(row, 4), lax.div(row, 4)
    x, zl, core = lax.div(col, 8), lax.rem(lax.div(col, 2), 4), lax.rem(col, 2)
    z = zh * 4 + zl

    def device(y=y, zh=zh, x=x, zl=zl, core=core):
        return (zh * 4 + y, (x * 4 + zl) * 2 + core)

    def turn(value, step, size=4):
        return lax.rem(value + step, size)

    def at_z(there):
        return device(zh=lax.div(there, 4), zl=lax.rem(there, 4))

    def at_y(there):
        return device(y=there)

    def at_x(there):
        return device(x=there)

    y_plus, y_minus = device(y=turn(y, 1)), device(y=turn(y, 3))
    x_plus, x_minus = device(x=turn(x, 1)), device(x=turn(x, 3))

    loads = []
    for block in range(4):
        at = pl.ds(block * B, B)
        loads.append((pan1_hbm.at[at, :], pan1.at[at, :]))
        loads.append((inv_hbm.at[:, at], inv.at[:, at]))
    loads += [(pan2_hbm, pan2), (link_hbm, link), (diag_hbm, diag), (marks_hbm, marks)]
    loads = [pltpu.make_async_copy(src, dst, load_sems.at[at]) for at, (src, dst) in enumerate(loads)]

    partner = device(core=1 - core)
    opposite = at_z(turn(z, 4, 8))
    def unless_me(there):
        return jnp.logical_not(jnp.logical_and(there[0] == row, there[1] == col))

    rows_to = (lax.div(col, 4), lax.rem(col, 4) * 8 + y * 2 + zh)
    rows_from = (lax.rem(col, 2) * 4 + lax.div(lax.rem(col, 8), 2), row * 4 + lax.div(col, 8))
    slice_to = (lax.rem(col, 8), row * 4 + lax.div(col, 8))
    slice_from = (lax.div(col, 4), lax.rem(col, 4) * 8 + row)
    rows_move, slice_move = unless_me(rows_to), unless_me(slice_to)

    barrier = pltpu.get_barrier_semaphore()

    def greet(there):
        pl.semaphore_signal(barrier, inc=1, device_id=there, device_id_type=MESH)

    loads[11].start()
    for step in (1, 2, 3):
        greet(at_y(turn(y, step)))
        greet(at_x(turn(x, step)))
        greet(device(x=turn(x, step), core=1 - core))
    greet(partner)
    for step in range(1, 8):
        greet(at_z(turn(z, step, 8)))

    @pl.when(rows_move)
    def _():
        greet(rows_from)

    @pl.when(slice_move)
    def _():
        greet(slice_from)

    for load in loads[0:8:2] + loads[1:8:2]:
        load.start()

    copies = Copies(send_sems, recv_sems)

    def permute(key, src, dst, there, moved):
        remote = copies.make(key, src, dst, there)
        local = pltpu.make_async_copy(src, dst, copies.recv_sem(key))

        @pl.when(moved)
        def _():
            remote.start()

        @pl.when(jnp.logical_not(moved))
        def _():
            local.start()

    for load in loads[0:8:2]:
        load.wait()

    block = pan1[pl.ds(pl.multiple_of(lax.div(col, 8) * B, B), B), :]
    turned[...] = block.T.reshape(8, H, B)
    loads[11].wait()
    first_own = marks[0, col].astype(F32)
    second_own = marks[1, col].astype(F32)
    early = []
    for block in range(4):
        at = slice(block * B, (block + 1) * B)
        scaled = pan1[at, :] * marks[0, row * 4 + block].astype(F32)
        high, low = split(scaled)
        for chunk in range(CH):
            lanes = slice(chunk * W, (chunk + 1) * W)
            pan1_cat[chunk, at, 0:W] = high[:, lanes]
            pan1_cat[chunk, at, W : 2 * W] = low[:, lanes]
        loads[2 * block + 1].wait()
        inv_high[:, at], inv_low[:, at] = split(inv[:, at])
        both = mul(inv_high[:, at], pan1_cat[0, at, :])
        rest = mul(inv_low[:, at], pan1_cat[0, at, 0:W])
        early.append(both[:, 0:W] + (both[:, W : 2 * W] + rest))
    total = ((early[0] + early[1]) + (early[2] + early[3])) * (-first_own)
    part[0] = total.reshape(4, 2, H, W)
    for load in loads[8:11]:
        load.start()

    def partial_product(chunk):
        both = mul(inv_high[...], pan1_cat[chunk])
        rest = mul(inv_low[...], pan1_cat[chunk, :, 0:W])
        total = (both[:, 0:W] + (both[:, W : 2 * W] + rest)) * (-first_own)
        part[chunk] = total.reshape(4, 2, H, W)

    scatter, gather, along_x, along_z, gather_x, gather_y = [], [], [], [], [], []
    for chunk in range(CH):
        for half in range(2):
            scatter.append(
                Exchange(
                    copies, ("part", chunk, half), y, 4, at_y,
                    lambda there, k=chunk, h=half: part.at[k, there, h],
                    lambda step, k=chunk, h=half: part_in.at[k, h, step - 1],
                    part_in.at[chunk, half],
                )
            )
            gather.append(
                Exchange(
                    copies, ("column", chunk, half), y, 4, at_y,
                    lambda there, k=chunk, h=half: column.at[k, y, h],
                    lambda step, k=chunk, h=half: column.at[k, y, h],
                    column.at[chunk, pl.ds(0, 3), half],
                )
            )
        along_x.append(
            Exchange(
                copies, ("slices", chunk), x * 2 + core, 8,
                lambda there: device(x=lax.div(there, 2), core=lax.rem(there, 2)),
                lambda there, k=chunk: pair.at[k, lax.rem(there, 2), jnp.minimum(lax.div(there, 2), 2)],
                lambda step, k=chunk: slices_in.at[k, step - 1],
                slices_in.at[chunk],
            )
        )
        along_z.append(
            Exchange(
                copies, ("depth", chunk), z, 8, at_z,
                lambda there, k=chunk: depth.at[k, z],
                lambda step, k=chunk: depth.at[k, z],
                depth.at[chunk, pl.ds(0, 7)],
            )
        )
        gather_x.append(
            Exchange(
                copies, ("grid_x", chunk), x, 4, at_x,
                lambda there, k=chunk: grid.at[k, core, y, :, x],
                lambda step, k=chunk: grid.at[k, core, y, :, x],
                grid.at[chunk, core, pl.ds(0, 3), :, 0],
            )
        )
        gather_y.append(
            Exchange(
                copies, ("grid_y", chunk), y, 4, at_y,
                lambda there, k=chunk: grid.at[k, core, y, :, pl.ds(0, 3)],
                lambda step, k=chunk: grid.at[k, core, y, :, pl.ds(0, 3)],
                grid.at[chunk, core, pl.ds(0, 3), :, pl.ds(0, 3)],
            )
        )
    across = Scatter(
        copies, "wide", x, x_plus, x_minus,
        lambda q, h: wide.at[q, pl.ds(2 * h, 2), core],
        lambda h: wide_relay.at[h],
        lambda h: wide_direct.at[h],
        lambda h: wide_final.at[h],
    )
    line = Exchange(
        copies, ("line", 0), zl, 4, lambda there: device(zl=there),
        lambda there: mine.at[there],
        lambda step: mine_in.at[step - 1],
        mine_in,
    )

    pl.semaphore_wait(barrier, 17 + jnp.where(rows_move, 1, 0) + jnp.where(slice_move, 1, 0))
    scatter[0].start()
    scatter[1].start()

    partial_product(1)
    scatter[2].start()
    scatter[3].start()
    partial_product(2)
    scatter[4].start()
    scatter[5].start()
    permute(("turned", 0), turned.at[lax.rem(col, 8)], turned_in, slice_to, slice_move)
    loads[8].wait()
    high, low = split(pan2[...] * second_own)
    pan2_cat[:, 0:B] = high
    pan2_cat[:, B : 2 * B] = low

    def wide_product(step):
        there = turn(x, step)
        at = pl.ds(pl.multiple_of(there * B, B), B)
        both = mul(inv_high[:, at], pan2_cat[...], ROWS)
        rest = mul(inv_low[:, at], pan2_cat[:, 0:B], ROWS)
        total = both[:, 0:B] + (both[:, B : 2 * B] + rest)
        wide[there] = total.reshape(4, 2, H, B)
        copies.send(("pairs", step), wide.at[there, :, 1 - core], wide_in.at[there], partner)

    def wide_ready(step):
        there = turn(x, step)
        copies.wait(("pairs", step), wide_in.at[there], partner)
        for lo in range(4):
            wide[there, lo, core] = wide[there, lo, core] + wide_in[there, lo]

    def to_opposite(chunk, half):
        scatter[2 * chunk + half].finish()
        quarter[chunk, half] = (part[chunk, y, half] + part_in[chunk, half, 0]) + (
            part_in[chunk, half, 1] + part_in[chunk, half, 2]
        )
        copies.send(("half", chunk, half), quarter.at[chunk, half], quarter_in.at[chunk, half], opposite)

    wide_product(2)
    to_opposite(0, 0)
    to_opposite(0, 1)
    wide_product(1)
    wide_ready(2)
    across.start_far()
    to_opposite(1, 0)
    to_opposite(1, 1)
    wide_product(3)
    wide_ready(1)
    across.start_plus()
    to_opposite(2, 0)
    to_opposite(2, 1)
    wide_product(0)
    wide_ready(3)
    across.start_minus()
    loads[9].wait()
    loads[10].wait()
    link_high[...], link_low[...] = split(link[...])
    for chunk in range(CH):
        for half in range(2):
            copies.wait(("half", chunk, half), quarter_in.at[chunk, half], opposite)
            column[chunk, y, half] = quarter[chunk, half] + quarter_in[chunk, half]
            gather[2 * chunk + half].start()

    copies.wait(("turned", 0), turned_in, partner)
    turned_high, turned_low = split(turned_in[...])

    for chunk in range(CH):
        gather[2 * chunk].finish()
        gather[2 * chunk + 1].finish()
        whole = column[chunk].reshape(B, W)
        column_first[:, chunk * W : (chunk + 1) * W] = whole
        whole = split(whole)
        slice_first = product((turned_high, turned_low), whole)
        both = mul(whole[0], pan2_cat[...], ROWS)
        rest = mul(whole[1], pan2_cat[:, 0:B], ROWS)
        cross[...] = both[:, 0:B] + (both[:, B : 2 * B] + rest)
        pair[chunk, 0] = slice_first.reshape(3, S, W)
        for third in range(3):
            pair[chunk, 1, third] = cross[pl.ds(pl.multiple_of(row * S, S), S), third * W : (third + 1) * W]
        along_x[chunk].start()
        if chunk == 0:
            wide_ready(0)
            across.relay()
    for chunk in range(CH):
        along_x[chunk].finish()
        total = pair[chunk, core, jnp.minimum(x, 2)] + slices_in[chunk, 0]
        for step in range(1, 7):
            total = total + slices_in[chunk, step]
        depth[chunk, z] = total
        along_z[chunk].start()

    for chunk in range(CH):
        along_z[chunk].finish()
        if chunk == 0:
            permute(("rows", 0), column.at[:, y, zh], link_rows, rows_to, rows_move)
        for half in range(2):
            grid[chunk, core, y, half, x] = (
                (depth[chunk, 4 * half] + depth[chunk, 4 * half + 1]) + depth[chunk, 4 * half + 2]
            ) + depth[chunk, 4 * half + 3]
        gather_x[chunk].start()

    def pass_on(chunk, step):
        part_at = grid.at[chunk, core, turn(y, step), :, pl.ds(0, 3)]
        copies.send(("swap", chunk), part_at, part_at, partner)

    for chunk in range(CH):
        gather_x[chunk].finish()
        gather_y[chunk].start()
        pass_on(chunk, 0)
    mine[0:2], mine[2:4] = across.finish()
    line.start()

    for chunk in range(CH):
        gather_y[chunk].finish()
        for step in (1, 3, 2):
            pass_on(chunk, step)

    line.finish()
    copies.wait(("rows", 0), link_rows, partner)
    block_row = row * 4 + lax.div(col, 8)
    rows_here = jnp.concatenate([link_rows[chunk] for chunk in range(CH)], axis=1)
    total = (mine[zl] + mine_in[0]) + (mine_in[1] + mine_in[2])
    total = total + product(split(rows_here), (link_high[...], link_low[...]))
    column_second[...] = total * (-marks[1, block_row].astype(F32))

    linked = []
    for chunk in range(CH):
        copies.wait(("swap", chunk), grid.at[chunk, 1 - core, :, :, pl.ds(0, 3)], partner)
        lanes = slice(chunk * W, (chunk + 1) * W)
        for piece in range(8):
            at = slice(piece * H, (piece + 1) * H)
            found = grid[chunk, 0, piece % 4, piece // 4, 0:3].reshape(H, W)
            diag_first[at, lanes] = diag[at, lanes] - found
        ready = split(diag_first[:, lanes])
        linked.append(product(ready, (link_high[lanes, :], link_low[lanes, :])))
    total = linked[0] + (linked[1] + linked[2])
    for chunk in range(CH):
        for piece in range(8):
            at = slice(chunk * W + piece * S, chunk * W + (piece + 1) * S)
            for third in range(3):
                lanes = slice(third * W, (third + 1) * W)
                corner[at, lanes] = -(total[at, lanes] + grid[chunk, 1, piece % 4, piece // 4, third])

    for kind, every in (
        ("part", part.at[:, pl.ds(0, 3)]),
        ("half", quarter),
        ("column", column.at[:, pl.ds(0, 3)]),
        ("pairs", wide_in),
        ("wide", wide.at[pl.ds(0, 3), :, 0]),
        ("line", mine_in),
        ("slices", slices_in),
        ("depth", depth.at[:, pl.ds(0, 7)]),
        ("grid_x", grid.at[:, 0, pl.ds(0, 3), :, 0]),
        ("grid_y", grid.at[:, 0, pl.ds(0, 3), :, pl.ds(0, 3)]),
        ("swap", grid.at[:, 0, :, :, pl.ds(0, 3)]),
    ):
        copies.sent(kind, every)

    @pl.when(slice_move)
    def _():
        copies.sent("turned", turned_in)

    @pl.when(rows_move)
    def _():
        copies.sent("rows", link_rows)


def deliver(*refs):
    sems = refs[-1]
    moves = [pltpu.make_async_copy(refs[at], refs[4 + at], sems.at[at]) for at in range(4)]
    for move in moves:
        move.start()
    for move in moves:
        move.wait()


def body(*arrays):
    *arrays, ancestors = arrays
    vmem = pl.BlockSpec(memory_space=pltpu.VMEM)
    hbm = pl.BlockSpec(memory_space=pltpu.HBM)
    shape = jax.ShapeDtypeStruct
    sizes = ((B, B), (B, B), (H, B), (B, B))
    held = pl.pallas_call(
        kernel,
        out_shape=tuple(pltpu.VMEM(size, F32) for size in sizes),
        in_specs=[hbm] * 6,
        out_specs=(vmem,) * 4,
        scratch_shapes=[
            pltpu.SMEM((2, 32), jnp.int32),
            pltpu.VMEM((B, 4 * B), F32),
            pltpu.VMEM((4 * B, B), F32),
            pltpu.VMEM((B, B), F32),
            pltpu.VMEM((B, B), F32),
            pltpu.VMEM((B, B), F32),
            pltpu.SemaphoreType.DMA((12,)),
            pltpu.VMEM((B, 4 * B), BF16),
            pltpu.VMEM((B, 4 * B), BF16),
            pltpu.VMEM((CH, 4 * B, 2 * W), BF16),
            pltpu.VMEM((B, 2 * B), BF16),
            pltpu.VMEM((B, B), BF16),
            pltpu.VMEM((B, B), BF16),
            pltpu.VMEM((CH, 4, 2, H, W), F32),
            pltpu.VMEM((CH, 2, 3, H, W), F32),
            pltpu.VMEM((CH, 2, H, W), F32),
            pltpu.VMEM((CH, 2, H, W), F32),
            pltpu.VMEM((CH, 4, 2, H, W), F32),
            pltpu.VMEM((4, 4, 2, H, B), F32),
            pltpu.VMEM((4, 4, H, B), F32),
            pltpu.VMEM((2, 2, H, B), F32),
            pltpu.VMEM((2, 2, H, B), F32),
            pltpu.VMEM((2, 2, H, B), F32),
            pltpu.VMEM((4, H, B), F32),
            pltpu.VMEM((3, H, B), F32),
            pltpu.VMEM((CH, H, W), F32),
            pltpu.VMEM((8, H, B), F32),
            pltpu.VMEM((H, B), F32),
            pltpu.VMEM((W, B), F32),
            pltpu.VMEM((CH, 2, 3, S, W), F32),
            pltpu.VMEM((CH, 7, S, W), F32),
            pltpu.VMEM((CH, 8, S, W), F32),
            pltpu.VMEM((CH, 2, 4, 2, 4, S, W), F32),
            pltpu.SemaphoreType.DMA((SENDS,)),
            pltpu.SemaphoreType.DMA((RECVS,)),
        ],
        compiler_params=pltpu.CompilerParams(
            collective_id=0, has_side_effects=True, vmem_limit_bytes=44 * 1024 * 1024
        ),
    )(*[pltpu.with_memory_space_constraint(given, pltpu.HBM) for given in (ancestors, *arrays)])
    held = [pltpu.with_memory_space_constraint(made, pltpu.VMEM) for made in held]
    return pl.pallas_call(
        deliver,
        out_shape=tuple(shape(size, F32) for size in sizes),
        in_specs=[vmem] * 4,
        out_specs=(hbm,) * 4,
        scratch_shapes=[pltpu.SemaphoreType.DMA((4,))],
    )(*held)


def solution(mesh):
    placed = (P("pcol", "prow"), P("prow", None), P("pcol", None), P(), P(), P())
    return jax.shard_map(
        body,
        mesh=mesh,
        in_specs=placed,
        out_specs=(P("pcol", None), P(), P(("prow", "pcol"), None), P()),
        check_vma=False,
    )
```
